32 devices in a mesh: grp: 2 (over x), seq: 8 (over z, y), ch: 2 (over core).
Axes of the slice: x: 2, y: 2, z: 4, core: 2. Of those that a mesh axis runs over, the one named last changes fastest.
Arguments:
- seq_in: bfloat16 [4096, 1536], P(('grp', 'seq'), 'ch'), parts along dimension 0, may hold values from -6 to 6
- conv_gain: float32 [2, 1536], P(None, 'ch'), may hold values from 0.5 to 1.5
- dw_kernel: float32 [2, 5, 1536], P(None, None, 'ch'), may hold values from -2.5 to 2.5
- mix_weight: bfloat16 [2, 1536, 1536], P(None, 'ch'), may hold values from -0.15625 to 0.15625
- attn_gain: float32 [1536], P('ch'), may hold values from 0.8 to 100, as said below
- q_weight: bfloat16 [1536, 1024], P(None, 'ch'), may hold values from -0.15625 to 0.15625
- kv_weight: bfloat16 [1536, 2, 256], P(None, None, 'ch'), may hold values from -0.15625 to 0.15625
- out_weight: bfloat16 [1024, 1536], P('ch'), may hold values from -0.1875 to 0.1875
Outputs:
- seq_out: bfloat16 [4096, 1536], P(('grp', 'seq'), 'ch'), parts along dimension 0
The draws below stay inside these ranges and needn't reach their ends.
There are 2 independent parts, one for each index of `grp`. The reference program is written for one: setup_inputs(seed, part) draws one part's arguments, and reference() takes and returns one part's arrays. A program takes and returns all parts, laid end to end along the dimension named above; an argument that names none is the same for every part. Nothing has to cross between parts.
Inputs may be any that keep to these rules, and one draw needn't show every extreme that they name: `attn_gain`: gains of the attention norm are positive.
All inputs are finite; a program needn't handle non-finite values.
Results may differ from the reference program's by a relative error of at most 0.03.
The reference program's roundings to bfloat16 on the way count: a program that leaves them out, or rounds other values in their place, can miss the bound.
Values may be sent and summed in bfloat16 or wider, within the bound.
No kernel may reach another device: no remote copies, remote signals or barrier semaphores. Data moves between devices by JAX's collectives and lax.ppermute only.
A program may use at most 64 MiB of HBM per device.

```python
import math
import jax
import jax.numpy as jnp
from jax import lax

C = 1536
HEADS = 8
KEY_VALUE_HEADS = 2
HD = 128
KW = 5
CONV_LAYERS = 2
FIRST_DILATION = 32
SECOND_DILATION = 64
LENGTH = 2048
QW = 1024
KVW = 256


def draw_attn_gain(key, part):
    first = jax.random.fold_in(key, 0)
    return (0.8 + 0.4 * jax.random.uniform(first, (C,), jnp.float32)).astype(jnp.float32)


def level_of(stream_key, dims, cuts, low, high):
    def one(axis_at, blocks):
        heights = jax.random.uniform(jax.random.fold_in(jax.random.fold_in(stream_key, 6), axis_at), (blocks,), jnp.float32, low / len(cuts), high / len(cuts))
        return jnp.repeat(jnp.exp(heights), dims[axis_at] // blocks).reshape((-1,) + (1,) * (len(dims) - axis_at - 1))

    level = one(*cuts[0])
    for cut in cuts[1:]:
        level = level * one(*cut)
    return level


def gaussian(rng, extent, scale, limit, pieces=(), kind=jnp.bfloat16):
    drawn = jax.random.normal(rng, extent, jnp.float32) * scale
    if len(pieces) > 0:
        drawn = level_of(rng, extent, pieces, -0.22, 0.18) * drawn
    return jnp.clip(drawn, min=-limit, max=limit).astype(kind)


def setup_inputs(seed: int = 0, part: int = 0) -> dict:
    key_of = jax.random.split(jax.random.key(seed), 9)
    own_keys = jax.random.split(jax.random.fold_in(key_of[8], part), 9)
    return {
        "seq_in": gaussian(own_keys[0], (LENGTH, C), 1.0, 6.0, ((0, 8), (1, 2))),
        "conv_gain": jnp.clip(1.0 + 0.1 * jax.random.normal(key_of[1], (CONV_LAYERS, C), jnp.float32), 0.5, 1.5),
        "dw_kernel": gaussian(key_of[2], (CONV_LAYERS, KW, C), KW ** -0.5, 2.5, ((2, 2),), jnp.float32),
        "mix_weight": gaussian(key_of[3], (CONV_LAYERS, C, C), C ** -0.5, 0.15625, ((1, 2),)),
        "attn_gain": draw_attn_gain(jax.random.fold_in(key_of[8], 71), part),
        "q_weight": gaussian(key_of[5], (C, QW), C ** -0.5, 0.15625, ((1, 2),)),
        "kv_weight": gaussian(key_of[6], (C, 2, KVW), C ** -0.5, 0.15625, ((2, 2),)),
        "out_weight": gaussian(key_of[7], (QW, C), QW ** -0.5, 0.1875, ((0, 2),)),
    }


EPSILON = 1e-06

def row_normalize(hidden, gain):
    return hidden * lax.rsqrt(lax.optimization_barrier(jnp.mean(hidden * hidden, axis=1, keepdims=True)) + EPSILON) * gain

def conv_layer(hidden, gain, kernels, weight, dilation):
    length_rows = hidden.shape[0]
    normalized_rows = row_normalize(hidden, gain)
    reach = KW // 2 * dilation
    padded = jnp.pad(normalized_rows, ((reach, reach), (0, 0)))
    summed = padded[0:length_rows] * kernels[0]
    for tap_index in range(1, KW):
        summed = summed + padded[tap_index * dilation:tap_index * dilation + length_rows] * kernels[tap_index]
    gelu_output = jax.nn.gelu(summed, approximate=True).astype(jnp.bfloat16)
    return hidden + jnp.dot(gelu_output, weight, preferred_element_type=jnp.float32)

def reference(seq_in, conv_gain, dw_kernel, mix_weight, attn_gain, q_weight, kv_weight, out_weight):
    hidden = seq_in.astype(jnp.float32)
    dilation_list = [FIRST_DILATION, SECOND_DILATION]
    for layer_idx in range(CONV_LAYERS):
        hidden = conv_layer(hidden, conv_gain[layer_idx], dw_kernel[layer_idx], mix_weight[layer_idx], dilation_list[layer_idx])
    features = row_normalize(hidden, attn_gain).astype(jnp.bfloat16)
    group_size = HEADS // KEY_VALUE_HEADS
    query_rows = jnp.dot(features, q_weight, preferred_element_type=jnp.float32).astype(jnp.bfloat16)
    pairs = jnp.dot(features, kv_weight.reshape(C, 2 * KVW), preferred_element_type=jnp.float32).astype(jnp.bfloat16)
    keys_all = pairs[:, :KVW].reshape(LENGTH, KEY_VALUE_HEADS, HD).astype(jnp.float32)
    values_all = pairs[:, KVW:].reshape(LENGTH, KEY_VALUE_HEADS, HD).astype(jnp.float32)
    block_len = math.gcd(LENGTH, 256)
    query_blocks = query_rows.reshape(LENGTH // block_len, block_len, KEY_VALUE_HEADS, group_size, HD)
    scale = 1.0 / math.sqrt(HD)

    def attend(block):
        scores = jnp.einsum('pkgd,skd->kgps', block.astype(jnp.float32), keys_all) * scale
        peak = lax.optimization_barrier(jnp.max(scores, axis=-1, keepdims=True))
        probs = jnp.exp(scores - peak)
        totals = lax.optimization_barrier(jnp.sum(probs, axis=-1))
        weights = probs.astype(jnp.bfloat16).astype(jnp.float32)
        context = jnp.einsum('kgps,skd->kgpd', weights, values_all) / totals[..., None]
        context = jnp.transpose(context, (2, 0, 1, 3)).astype(jnp.bfloat16)
        return context.reshape(block_len, QW)
    attended = lax.map(attend, query_blocks).reshape(LENGTH, QW)
    mixed = jnp.dot(attended, out_weight, preferred_element_type=jnp.float32)
    return (hidden + mixed).astype(jnp.bfloat16)
```

```python
import functools
import math

import jax
import jax.numpy as jnp
from jax import lax
from jax.experimental import pallas as pl
from jax.experimental.pallas import tpu as pltpu
from jax.sharding import PartitionSpec as P

HD = 128
EPSILON = 1e-06
BF16 = jnp.bfloat16
F32 = jnp.float32
SWAP = [(0, 1), (1, 0)]
VMEM = pl.BlockSpec(memory_space=pltpu.VMEM)
SMEM = pl.BlockSpec(memory_space=pltpu.SMEM)
ANY = pl.BlockSpec(memory_space=pl.ANY)


def peer(array):
    return lax.ppermute(array, "ch", SWAP)


def ring_order(count):
    width = 1
    while width * width * 4 <= count:
        width *= 2
    rows = count // width
    if width == 1 or rows * width != count:
        return list(range(count))
    order = [row * width for row in range(rows)]
    for step, row in enumerate(reversed(range(rows))):
        columns = range(1, width) if step % 2 == 0 else range(width - 1, 0, -1)
        order += [row * width + column for column in columns]
    return order


def tower_kernel(
    place, x_own, x_peer, near_own, near_peer, far_own, far_peer, small_own, small_peer, mix_own, mix_peer,
    features, hidden_own, hidden_peer,
    wide, normed, middle, act, small, weights, sems,
    *, rows, first, second, length, taps,
):
    own = place[0]
    other = 1 - own
    half_taps = taps // 2
    reach1 = half_taps * second
    reach = half_taps * first + reach1
    mine = rows // 2
    lead = mine + 2 * reach1
    span = mine + 2 * reach
    width = x_own.shape[1]
    channels = 2 * width

    copies = []
    for layer in range(2):
        for side, source in ((own, mix_own), (other, mix_peer)):
            copy = pltpu.make_async_copy(source.at[layer], weights.at[layer, side], sems.at[layer, 0 if source is mix_own else 1])
            copy.start()
            copies.append(copy)

    near_at = pl.multiple_of(place[2], 64)
    far_at = pl.multiple_of(place[3], 64)
    for side, body, near, far, params in (
        (own, x_own, near_own, far_own, small_own),
        (other, x_peer, near_peer, far_peer, small_peer),
    ):
        wide[side, pl.ds(reach, rows), :] = body[...]
        wide[side, pl.ds(near_at, reach), :] = near[...]
        wide[side, pl.ds(far_at, reach), :] = far[...]
        small[side] = params[...]

    shift = pl.multiple_of(own * mine, 64)
    start = place[1] + own * mine
    chunk = 64

    def scale_of(parts, first_position):
        squares = jnp.sum(parts[0] * parts[0], axis=1, keepdims=True) + jnp.sum(parts[1] * parts[1], axis=1, keepdims=True)
        scale = lax.rsqrt(squares / channels + EPSILON)
        if first_position is None:
            return scale
        position = first_position + lax.broadcasted_iota(jnp.int32, scale.shape, 0)
        return jnp.where((position >= 0) & (position < length), scale, 0.0)

    def norm0(i, carry):
        at = pl.multiple_of(i * chunk, chunk)
        parts = [wide[h, pl.ds(pl.multiple_of(shift + at, 64), chunk), :].astype(F32) for h in range(2)]
        scale = scale_of(parts, start - reach + at)
        for h in range(2):
            normed[h, pl.ds(at, chunk), :] = parts[h] * scale * small[h, 0:1, :]
        return carry

    lax.fori_loop(0, span // chunk, norm0, 0)

    def convolve(layer, count, dilation):
        block = 32
        strip = 256

        def body(i, carry):
            at = pl.multiple_of(i * block, block)
            for h in range(2):
                for column in range(0, width, strip):
                    cols = pl.ds(column, strip)
                    total = None
                    for tap in range(taps):
                        kernel = small[h, pl.ds(2 + layer * taps + tap, 1), cols]
                        term = normed[h, pl.ds(pl.multiple_of(at + tap * dilation, 32), block), cols] * kernel
                        total = term if total is None else total + term
                    act[h, pl.ds(at, block), cols] = jax.nn.gelu(total, approximate=True).astype(BF16)
            return carry

        lax.fori_loop(0, count // block, body, 0)

    convolve(0, lead, first)
    copies[0].wait()
    copies[1].wait()
    for h in range(2):
        cols = pl.ds(h * width, width)
        mixed = jnp.dot(act[0, 0:lead, :], weights[0, 0, :, cols], preferred_element_type=F32)
        mixed = mixed + jnp.dot(act[1, 0:lead, :], weights[0, 1, :, cols], preferred_element_type=F32)
        before = wide[h, pl.ds(pl.multiple_of(shift + reach - reach1, 32), lead), :].astype(F32)
        middle[h] = before + mixed

    def norm1(i, carry):
        at = pl.multiple_of(i * chunk, chunk)
        parts = [middle[h, pl.ds(at, chunk), :] for h in range(2)]
        scale = scale_of(parts, start - reach1 + at)
        for h in range(2):
            normed[h, pl.ds(at, chunk), :] = parts[h] * scale * small[h, 1:2, :]
        return carry

    lax.fori_loop(0, lead // chunk, norm1, 0)
    convolve(1, mine, second)
    copies[2].wait()
    copies[3].wait()
    parts = []
    for h in range(2):
        cols = pl.ds(h * width, width)
        mixed = jnp.dot(act[0, 0:mine, :], weights[1, 0, :, cols], preferred_element_type=F32)
        mixed = mixed + jnp.dot(act[1, 0:mine, :], weights[1, 1, :, cols], preferred_element_type=F32)
        middle[h, pl.ds(reach1, mine), :] = middle[h, pl.ds(reach1, mine), :] + mixed
    hidden_own[...] = middle[own, pl.ds(reach1, mine), :]
    hidden_peer[...] = middle[other, pl.ds(reach1, mine), :]
    parts = [middle[h, pl.ds(reach1, mine), :] for h in range(2)]
    scale = scale_of(parts, None)
    for h in range(2):
        features[:, h * width : (h + 1) * width] = (parts[h] * scale * small[h, pl.ds(2 + 2 * taps, 1), :]).astype(BF16)


def project_kernel(place, own_ref, peer_ref, weight, out):
    count = own_ref.shape[0]
    at = pl.multiple_of(place[0] * count, count)
    back = pl.multiple_of((1 - place[0]) * count, count)
    out[pl.ds(at, count), :] = jnp.dot(own_ref[...], weight[...], preferred_element_type=F32).astype(BF16)
    out[pl.ds(back, count), :] = jnp.dot(peer_ref[...], weight[...], preferred_element_type=F32).astype(BF16)


def attend_kernel(q_ref, *refs, scale):
    blocks, out = refs[:-1], refs[-1]
    factor = scale * math.log2(math.e)
    heads = q_ref.shape[1] // HD
    for head in range(heads):
        q = q_ref[:, head * HD : (head + 1) * HD]
        scores = [
            lax.dot_general(q, kv[:, 0:HD], (((1,), (1,)), ((), ())), preferred_element_type=F32) for kv in blocks
        ]
        peak = functools.reduce(jnp.maximum, [jnp.max(s, axis=1, keepdims=True) for s in scores])
        total = None
        context = None
        for s, kv in zip(scores, blocks):
            probs = jnp.exp2((s - peak) * factor)
            part = jnp.sum(probs, axis=1, keepdims=True)
            value = jnp.dot(probs.astype(BF16), kv[:, HD:], preferred_element_type=F32)
            total = part if total is None else total + part
            context = value if context is None else context + value
        out[:, head * HD : (head + 1) * HD] = (context / total).astype(BF16)


def finish_kernel(place, ctx_own, ctx_peer, w_own, w_peer, hid_own, hid_peer, out):
    count = hid_own.shape[0]
    width = hid_own.shape[1]
    cols = pl.ds(pl.multiple_of(place[0] * width, 128), width)
    for at, hid in ((place[0] * count, hid_own), ((1 - place[0]) * count, hid_peer)):
        rows = pl.ds(pl.multiple_of(at, count), count)
        mixed = jnp.dot(ctx_own[rows, :], w_own[:, cols], preferred_element_type=F32)
        mixed = mixed + jnp.dot(ctx_peer[rows, :], w_peer[...], preferred_element_type=F32)
        out[rows, :] = (hid[...] + mixed).astype(BF16)


def params(limit=100 << 20):
    return pltpu.CompilerParams(vmem_limit_bytes=56 << 20)


def local(seq_in, conv_gain, dw_kernel, mix_weight, attn_gain, q_weight, kv_weight, out_weight):
    rows, width = seq_in.shape
    taps = dw_kernel.shape[1]
    size = lax.axis_size("seq")
    me = lax.axis_index("seq")
    core = lax.axis_index("ch")
    first, second = rows // 8, rows // 4
    reach1 = taps // 2 * second
    reach = taps // 2 * first + reach1
    mine = rows // 2
    lead = mine + 2 * reach1
    span = mine + 2 * reach

    even = me % 2 == 0
    low, high = seq_in[:reach], seq_in[rows - reach :]
    near_pairs = [(i, i ^ 1) for i in range(size)]
    far_pairs = [(0, 0), (size - 1, size - 1)]
    for i in range(1, size - 1, 2):
        far_pairs += [(i, i + 1), (i + 1, i)]
    near = lax.ppermute(jnp.where(even, high, low), "seq", near_pairs)
    far = lax.ppermute(jnp.where(even, low, high), "seq", far_pairs)

    small = jnp.concatenate(
        [conv_gain, dw_kernel.reshape(2 * taps, width), attn_gain[None, :], jnp.zeros((3, width), F32)], axis=0
    )
    small_peer = peer(small)
    x_peer = peer(seq_in)
    mix_peer = peer(mix_weight)
    out_away = lax.dynamic_slice_in_dim(out_weight, (1 - core) * width, width, axis=1)
    out_peer = peer(out_away)
    near_peer = peer(near)
    far_peer = peer(far)

    bottom = rows + reach
    place = jnp.stack(
        [core, me * rows, jnp.where(even, bottom, 0), jnp.where(even, 0, bottom)]
    ).astype(jnp.int32)

    features, hidden_own, hidden_away = pl.pallas_call(
        functools.partial(
            tower_kernel, rows=rows, first=first, second=second, length=rows * size, taps=taps
        ),
        out_shape=(
            jax.ShapeDtypeStruct((mine, 2 * width), BF16),
            jax.ShapeDtypeStruct((mine, width), F32),
            jax.ShapeDtypeStruct((mine, width), F32),
        ),
        in_specs=[SMEM] + [VMEM] * 8 + [ANY] * 2,
        out_specs=(VMEM, VMEM, VMEM),
        scratch_shapes=[
            pltpu.VMEM((2, rows + 2 * reach, width), BF16),
            pltpu.VMEM((2, span, width), F32),
            pltpu.VMEM((2, lead, width), F32),
            pltpu.VMEM((2, lead, width), BF16),
            pltpu.VMEM((2,) + small.shape, F32),
            pltpu.VMEM((2, 2, width, 2 * width), BF16),
            pltpu.SemaphoreType.DMA((2, 2)),
        ],
        compiler_params=params(),
        name="tower",
    )(place, seq_in, x_peer, near, near_peer, far, far_peer, small, small_peer, mix_weight, mix_peer)

    features_peer = peer(features)
    kv_width = 2 * kv_weight.shape[2]

    def project(weight, name):
        return pl.pallas_call(
            project_kernel,
            out_shape=jax.ShapeDtypeStruct((rows, weight.shape[1]), BF16),
            in_specs=[SMEM, VMEM, VMEM, VMEM],
            out_specs=VMEM,
            compiler_params=params(),
            name=name,
        )(place, features, features_peer, weight)

    kv = project(kv_weight.reshape(2 * width, kv_width), "keyvalue")
    order = ring_order(size)
    ahead = [(order[i], order[(i + 1) % size]) for i in range(size)]
    behind = [(b, a) for a, b in ahead]
    blocks = [kv]
    up = down = kv
    for step in range(size // 2):
        up = lax.ppermute(up, "seq", ahead)
        blocks.append(up)
        if 2 * step + 2 < size:
            down = lax.ppermute(down, "seq", behind)
            blocks.append(down)
    hidden_peer = peer(hidden_away)
    queries = project(q_weight, "query")
    context = pl.pallas_call(
        functools.partial(attend_kernel, scale=1.0 / math.sqrt(HD)),
        out_shape=jax.ShapeDtypeStruct(queries.shape, BF16),
        in_specs=[VMEM] * (1 + len(blocks)),
        out_specs=VMEM,
        compiler_params=params(),
        name="attend",
    )(queries, *blocks)
    context_peer = peer(context)
    return pl.pallas_call(
        finish_kernel,
        out_shape=jax.ShapeDtypeStruct((rows, width), BF16),
        in_specs=[SMEM] + [VMEM] * 6,
        out_specs=VMEM,
        compiler_params=params(),
        name="finish",
    )(place, context, context_peer, out_weight, out_peer, hidden_own, hidden_peer)


def solution(mesh):
    return jax.shard_map(
        local,
        mesh=mesh,
        in_specs=(
            P(("grp", "seq"), "ch"),
            P(None, "ch"),
            P(None, None, "ch"),
            P(None, "ch", None),
            P("ch"),
            P(None, "ch"),
            P(None, None, "ch"),
            P("ch", None),
        ),
        out_specs=P(("grp", "seq"), "ch"),
        check_vma=False,
    )
```

```python
import functools
import math

import jax
import jax.numpy as jnp
from jax import lax
from jax.experimental import pallas as pl
from jax.experimental.pallas import tpu as pltpu
from jax.sharding import PartitionSpec as P

HD = 128
EPSILON = 1e-06
BF16 = jnp.bfloat16
F32 = jnp.float32
SWAP = [(0, 1), (1, 0)]
VMEM = pl.BlockSpec(memory_space=pltpu.VMEM)
SMEM = pl.BlockSpec(memory_space=pltpu.SMEM)
ANY = pl.BlockSpec(memory_space=pl.ANY)


def peer(array):
    return lax.ppermute(array, "ch", SWAP)


def ring_order(count):
    width = 1
    while width * width * 4 <= count:
        width *= 2
    rows = count // width
    if width == 1 or rows * width != count:
        return list(range(count))
    order = [row * width for row in range(rows)]
    for step, row in enumerate(reversed(range(rows))):
        columns = range(1, width) if step % 2 == 0 else range(width - 1, 0, -1)
        order += [row * width + column for column in columns]
    return order


def tower_kernel(
    place, x_own, x_peer, near_own, near_peer, far_own, far_peer, small_own, small_peer, mix_own, mix_peer,
    features, hidden_own, hidden_peer,
    wide, normed, middle, act, small, weights, sems,
    *, rows, first, second, length, taps,
):
    own = place[0]
    other = 1 - own
    half_taps = taps // 2
    reach1 = half_taps * second
    reach = half_taps * first + reach1
    mine = rows // 2
    lead = mine + 2 * reach1
    span = mine + 2 * reach
    width = x_own.shape[1]
    channels = 2 * width

    copies = []
    for layer in range(2):
        for side, source in ((own, mix_own), (other, mix_peer)):
            copy = pltpu.make_async_copy(source.at[layer], weights.at[layer, side], sems.at[layer, 0 if source is mix_own else 1])
            copy.start()
            copies.append(copy)

    near_at = pl.multiple_of(place[2], 64)
    far_at = pl.multiple_of(place[3], 64)
    for side, body, near, far, params in (
        (own, x_own, near_own, far_own, small_own),
        (other, x_peer, near_peer, far_peer, small_peer),
    ):
        wide[side, pl.ds(reach, rows), :] = body[...]
        wide[side, pl.ds(near_at, reach), :] = near[...]
        wide[side, pl.ds(far_at, reach), :] = far[...]
        small[side] = params[...]

    shift = pl.multiple_of(own * mine, 64)
    start = place[1] + own * mine
    chunk = 64

    def scale_of(parts, first_position):
        squares = jnp.sum(parts[0] * parts[0], axis=1, keepdims=True) + jnp.sum(parts[1] * parts[1], axis=1, keepdims=True)
        scale = lax.rsqrt(squares / channels + EPSILON)
        if first_position is None:
            return scale
        position = first_position + lax.broadcasted_iota(jnp.int32, scale.shape, 0)
        return jnp.where((position >= 0) & (position < length), scale, 0.0)

    def norm0(i, carry):
        at = pl.multiple_of(i * chunk, chunk)
        parts = [wide[h, pl.ds(pl.multiple_of(shift + at, 64), chunk), :].astype(F32) for h in range(2)]
        scale = scale_of(parts, start - reach + at)
        for h in range(2):
            normed[h, pl.ds(at, chunk), :] = parts[h] * scale * small[h, 0:1, :]
        return carry

    lax.fori_loop(0, span // chunk, norm0, 0)

    def convolve(layer, count, dilation):
        block = 32
        strip = 256

        def body(i, carry):
            at = pl.multiple_of(i * block, block)
            for h in range(2):
                for column in range(0, width, strip):
                    cols = pl.ds(column, strip)
                    total = None
                    for tap in range(taps):
                        kernel = small[h, pl.ds(2 + layer * taps + tap, 1), cols]
                        term = normed[h, pl.ds(pl.multiple_of(at + tap * dilation, 32), block), cols] * kernel
                        total = term if total is None else total + term
                    act[h, pl.ds(at, block), cols] = jax.nn.gelu(total, approximate=True).astype(BF16)
            return carry

        lax.fori_loop(0, count // block, body, 0)

    convolve(0, lead, first)
    copies[0].wait()
    copies[1].wait()
    for h in range(2):
        cols = pl.ds(h * width, width)
        mixed = jnp.dot(act[0, 0:lead, :], weights[0, 0, :, cols], preferred_element_type=F32)
        mixed = mixed + jnp.dot(act[1, 0:lead, :], weights[0, 1, :, cols], preferred_element_type=F32)
        before = wide[h, pl.ds(pl.multiple_of(shift + reach - reach1, 32), lead), :].astype(F32)
        middle[h] = before + mixed

    def norm1(i, carry):
        at = pl.multiple_of(i * chunk, chunk)
        parts = [middle[h, pl.ds(at, chunk), :] for h in range(2)]
        scale = scale_of(parts, start - reach1 + at)
        for h in range(2):
            normed[h, pl.ds(at, chunk), :] = parts[h] * scale * small[h, 1:2, :]
        return carry

    lax.fori_loop(0, lead // chunk, norm1, 0)
    convolve(1, mine, second)
    copies[2].wait()
    copies[3].wait()
    parts = []
    for h in range(2):
        cols = pl.ds(h * width, width)
        mixed = jnp.dot(act[0, 0:mine, :], weights[1, 0, :, cols], preferred_element_type=F32)
        mixed = mixed + jnp.dot(act[1, 0:mine, :], weights[1, 1, :, cols], preferred_element_type=F32)
        middle[h, pl.ds(reach1, mine), :] = middle[h, pl.ds(reach1, mine), :] + mixed
    hidden_own[...] = middle[own, pl.ds(reach1, mine), :]
    hidden_peer[...] = middle[other, pl.ds(reach1, mine), :]
    parts = [middle[h, pl.ds(reach1, mine), :] for h in range(2)]
    scale = scale_of(parts, None)
    for h in range(2):
        features[:, h * width : (h + 1) * width] = (parts[h] * scale * small[h, pl.ds(2 + 2 * taps, 1), :]).astype(BF16)


def project_kernel(place, own_ref, peer_ref, weight, out):
    count = own_ref.shape[0]
    at = pl.multiple_of(place[0] * count, count)
    back = pl.multiple_of((1 - place[0]) * count, count)
    out[pl.ds(at, count), :] = jnp.dot(own_ref[...], weight[...], preferred_element_type=F32).astype(BF16)
    out[pl.ds(back, count), :] = jnp.dot(peer_ref[...], weight[...], preferred_element_type=F32).astype(BF16)


def attend_kernel(*refs, count, scale, first, last):
    q_ref, blocks, refs = refs[0], refs[1 : 1 + count], refs[1 + count :]
    state_in, refs = ((), refs) if first else (refs[:2], refs[2:])
    factor = scale * math.log2(math.e)
    heads = q_ref.shape[1] // HD
    for head in range(heads):
        cols = slice(head * HD, (head + 1) * HD)
        q = q_ref[:, cols]
        scores = [
            lax.dot_general(q, kv[:, 0:HD], (((1,), (1,)), ((), ())), preferred_element_type=F32) for kv in blocks
        ]
        peaks = [jnp.max(s, axis=1, keepdims=True) for s in scores]
        total = None
        context = None
        if not first:
            stats, summed = state_in
            before = stats[:, head : head + 1]
            peaks.append(before)
        peak = functools.reduce(jnp.maximum, peaks)
        if not first:
            keep = jnp.exp2((before - peak) * factor)
            total = stats[:, heads + head : heads + head + 1] * keep
            context = summed[:, cols] * keep
        for s, kv in zip(scores, blocks):
            probs = jnp.exp2((s - peak) * factor)
            part = jnp.sum(probs, axis=1, keepdims=True)
            value = jnp.dot(probs.astype(BF16), kv[:, HD:], preferred_element_type=F32)
            total = part if total is None else total + part
            context = value if context is None else context + value
        if last:
            refs[0][:, cols] = (context / total).astype(BF16)
        else:
            refs[0][:, head : head + 1] = peak
            refs[0][:, heads + head : heads + head + 1] = total
            refs[1][:, cols] = context


def begin_kernel(place, ctx, w_own, hid_own, hid_peer, out):
    count, width = hid_own.shape
    cols = pl.ds(pl.multiple_of(place[0] * width, 128), width)
    for at, hid in ((place[0] * count, hid_own), ((1 - place[0]) * count, hid_peer)):
        rows = pl.ds(pl.multiple_of(at, count), count)
        out[rows, :] = hid[...] + jnp.dot(ctx[rows, :], w_own[:, cols], preferred_element_type=F32)


def finish_kernel(place, ctx, w_peer, partial, out):
    width = partial.shape[1]
    cols = pl.ds(pl.multiple_of(place[0] * width, 128), width)
    mixed = jnp.dot(ctx[...], w_peer[:, cols], preferred_element_type=F32)
    out[...] = (partial[...] + mixed).astype(BF16)


def call(kernel, outs, name, mebibytes, *operands, specs=None, scratch=(), hbm_out=False):
    held, in_specs = [], []
    for i, operand in enumerate(operands):
        spec = (specs or {}).get(i, VMEM)
        in_specs.append(spec)
        space = pltpu.VMEM if spec is VMEM else pltpu.HBM if spec is ANY else None
        held.append(pltpu.with_memory_space_constraint(operand, space) if space else operand)
    shapes = tuple((jax.ShapeDtypeStruct if hbm_out else pltpu.VMEM)(shape, dtype) for shape, dtype in outs)
    result = pl.pallas_call(
        kernel,
        out_shape=shapes,
        in_specs=in_specs,
        out_specs=(VMEM,) * len(shapes),
        scratch_shapes=list(scratch),
        compiler_params=pltpu.CompilerParams(vmem_limit_bytes=mebibytes << 20),
        name=name,
    )(*held)
    return result if len(outs) > 1 else result[0]


def local(seq_in, conv_gain, dw_kernel, mix_weight, attn_gain, q_weight, kv_weight, out_weight):
    rows, width = seq_in.shape
    taps = dw_kernel.shape[1]
    size = lax.axis_size("seq")
    me = lax.axis_index("seq")
    core = lax.axis_index("ch")
    first, second = rows // 8, rows // 4
    reach1 = taps // 2 * second
    reach = taps // 2 * first + reach1
    mine = rows // 2
    lead = mine + 2 * reach1
    span = mine + 2 * reach

    even = me % 2 == 0
    low, high = seq_in[:reach], seq_in[rows - reach :]
    near_pairs = [(i, i ^ 1) for i in range(size)]
    far_pairs = [(0, 0), (size - 1, size - 1)]
    for i in range(1, size - 1, 2):
        far_pairs += [(i, i + 1), (i + 1, i)]
    to_near, to_far, x_sent, mix_sent, out_sent = lax.optimization_barrier(
        (jnp.where(even, high, low), jnp.where(even, low, high), seq_in, mix_weight, out_weight)
    )
    near = lax.ppermute(to_near, "seq", near_pairs)
    far = lax.ppermute(to_far, "seq", far_pairs)

    small = jnp.concatenate(
        [conv_gain, dw_kernel.reshape(2 * taps, width), attn_gain[None, :], jnp.zeros((3, width), F32)], axis=0
    )
    small_peer = peer(small)
    x_peer = peer(x_sent)
    mix_peer = peer(mix_sent)
    out_peer = peer(out_sent)
    bottom = rows + reach
    place = jnp.stack(
        [core, me * rows, jnp.where(even, bottom, 0), jnp.where(even, 0, bottom)]
    ).astype(jnp.int32)
    kv_flat = kv_weight.reshape(2 * width, 2 * kv_weight.shape[2])
    near, far, small, small_peer, x_peer, place, kv_flat = lax.optimization_barrier(
        (near, far, small, small_peer, x_peer, place, kv_flat)
    )
    near_peer = peer(near)
    far_peer = peer(far)

    features, hidden_own, hidden_away = call(
        functools.partial(
            tower_kernel, rows=rows, first=first, second=second, length=rows * size, taps=taps
        ),
        [((mine, 2 * width), BF16), ((mine, width), F32), ((mine, width), F32)],
        "tower",
        24,
        place, seq_in, x_peer, near, near_peer, far, far_peer, small, small_peer, mix_weight, mix_peer,
        specs={0: SMEM, 9: ANY, 10: ANY},
        scratch=[
            pltpu.VMEM((2, rows + 2 * reach, width), BF16),
            pltpu.VMEM((2, span, width), F32),
            pltpu.VMEM((2, lead, width), F32),
            pltpu.VMEM((2, lead, width), BF16),
            pltpu.VMEM((2,) + small.shape, F32),
            pltpu.VMEM((2, 2, width, 2 * width), BF16),
            pltpu.SemaphoreType.DMA((2, 2)),
        ],
    )

    features_peer = peer(features)

    def project(weight, name):
        return call(
            project_kernel, [((rows, weight.shape[1]), BF16)], name, 4, place, features, features_peer, weight,
            specs={0: SMEM},
        )

    kv = project(kv_flat, "keyvalue")
    order = ring_order(size)
    ahead = [(order[i], order[(i + 1) % size]) for i in range(size)]
    behind = [(b, a) for a, b in ahead]
    queries = None
    heads = q_weight.shape[1] // HD
    state = ()
    fresh = [kv]
    up = down = kv
    for step in range(size // 2):
        up = lax.ppermute(up, "seq", ahead)
        arrived = [up]
        if 2 * step + 2 < size:
            down = lax.ppermute(down, "seq", behind)
            arrived.append(down)
        if queries is None:
            queries = project(q_weight, "query")
            hidden_peer = peer(hidden_away)
        state = call(
            functools.partial(attend_kernel, count=len(fresh), scale=1.0 / math.sqrt(HD), first=step == 0, last=False),
            [((rows, HD), F32), ((rows, heads * HD), F32)],
            "attend%d" % step,
            8,
            queries, *fresh, *state,
        )
        if step + 1 < size // 2:
            up, down, *state = lax.optimization_barrier((up, down, *state))
            arrived = [up, down]
        fresh = arrived
    context = call(
        functools.partial(attend_kernel, count=len(fresh), scale=1.0 / math.sqrt(HD), first=False, last=True),
        [((rows, heads * HD), BF16)],
        "attend_last",
        8,
        queries, *fresh, *state,
    )
    context_peer = peer(context)
    partial = call(
        begin_kernel, [((rows, width), F32)], "begin", 8, place, context, out_weight, hidden_own, hidden_peer, specs={0: SMEM}
    )
    return call(
        finish_kernel, [((rows, width), BF16)], "finish", 8, place, context_peer, out_peer, partial,
        specs={0: SMEM}, hbm_out=True,
    )


def solution(mesh):
    return jax.shard_map(
        local,
        mesh=mesh,
        in_specs=(
            P(("grp", "seq"), "ch"),
            P(None, "ch"),
            P(None, None, "ch"),
            P(None, "ch", None),
            P("ch"),
            P(None, "ch"),
            P(None, None, "ch"),
            P("ch", None),
        ),
        out_specs=P(("grp", "seq"), "ch"),
        check_vma=False,
    )
```

```python
import functools
import math

import jax
import jax.numpy as jnp
from jax import lax
from jax.experimental import pallas as pl
from jax.experimental.pallas import tpu as pltpu
from jax.sharding import PartitionSpec as P

HD = 128
EPSILON = 1e-06
BF16 = jnp.bfloat16
F32 = jnp.float32
SWAP = [(0, 1), (1, 0)]
VMEM = pl.BlockSpec(memory_space=pltpu.VMEM)
SMEM = pl.BlockSpec(memory_space=pltpu.SMEM)
ANY = pl.BlockSpec(memory_space=pl.ANY)


def peer(array):
    return lax.ppermute(array, "ch", SWAP)


def ring_order(count):
    width = 1
    while width * width * 4 <= count:
        width *= 2
    rows = count // width
    if width == 1 or rows * width != count:
        return list(range(count))
    order = [row * width for row in range(rows)]
    for step, row in enumerate(reversed(range(rows))):
        columns = range(1, width) if step % 2 == 0 else range(width - 1, 0, -1)
        order += [row * width + column for column in columns]
    return order


def tower_kernel(
    place, x_own, x_peer, near_own, near_peer, far_own, far_peer, small_own, small_peer, mix_own, mix_peer,
    features, hidden_own, hidden_peer,
    wide, normed, middle, act, small, weights, sems,
    *, rows, first, second, length, taps,
):
    own = place[0]
    other = 1 - own
    half_taps = taps // 2
    reach1 = half_taps * second
    reach = half_taps * first + reach1
    mine = rows // 2
    lead = mine + 2 * reach1
    span = mine + 2 * reach
    width = x_own.shape[1]
    channels = 2 * width

    copies = []
    for layer in range(2):
        for side, source in ((own, mix_own), (other, mix_peer)):
            copy = pltpu.make_async_copy(source.at[layer], weights.at[layer, side], sems.at[layer, 0 if source is mix_own else 1])
            copy.start()
            copies.append(copy)

    near_at = pl.multiple_of(place[2], 64)
    far_at = pl.multiple_of(place[3], 64)
    for side, body, near, far, params in (
        (own, x_own, near_own, far_own, small_own),
        (other, x_peer, near_peer, far_peer, small_peer),
    ):
        wide[side, pl.ds(reach, rows), :] = body[...]
        wide[side, pl.ds(near_at, reach), :] = near[...]
        wide[side, pl.ds(far_at, reach), :] = far[...]
        small[side] = params[...]

    shift = pl.multiple_of(own * mine, 64)
    start = place[1] + own * mine
    chunk = 64

    def scale_of(parts, first_position):
        squares = jnp.sum(parts[0] * parts[0], axis=1, keepdims=True) + jnp.sum(parts[1] * parts[1], axis=1, keepdims=True)
        scale = lax.rsqrt(squares / channels + EPSILON)
        if first_position is None:
            return scale
        position = first_position + lax.broadcasted_iota(jnp.int32, scale.shape, 0)
        return jnp.where((position >= 0) & (position < length), scale, 0.0)

    def norm0(i, carry):
        at = pl.multiple_of(i * chunk, chunk)
        parts = [wide[h, pl.ds(pl.multiple_of(shift + at, 64), chunk), :].astype(F32) for h in range(2)]
        scale = scale_of(parts, start - reach + at)
        for h in range(2):
            normed[h, pl.ds(at, chunk), :] = parts[h] * scale * small[h, 0:1, :]
        return carry

    lax.fori_loop(0, span // chunk, norm0, 0)

    def convolve(layer, count, dilation):
        block = 32
        strip = 256

        def body(i, carry):
            at = pl.multiple_of(i * block, block)
            for h in range(2):
                for column in range(0, width, strip):
                    cols = pl.ds(column, strip)
                    total = None
                    for tap in range(taps):
                        kernel = small[h, pl.ds(2 + layer * taps + tap, 1), cols]
                        term = normed[h, pl.ds(pl.multiple_of(at + tap * dilation, 32), block), cols] * kernel
                        total = term if total is None else total + term
                    act[h, pl.ds(at, block), cols] = jax.nn.gelu(total, approximate=True).astype(BF16)
            return carry

        lax.fori_loop(0, count // block, body, 0)

    convolve(0, lead, first)
    copies[0].wait()
    copies[1].wait()
    for h in range(2):
        cols = pl.ds(h * width, width)
        mixed = jnp.dot(act[0, 0:lead, :], weights[0, 0, :, cols], preferred_element_type=F32)
        mixed = mixed + jnp.dot(act[1, 0:lead, :], weights[0, 1, :, cols], preferred_element_type=F32)
        before = wide[h, pl.ds(pl.multiple_of(shift + reach - reach1, 32), lead), :].astype(F32)
        middle[h] = before + mixed

    def norm1(i, carry):
        at = pl.multiple_of(i * chunk, chunk)
        parts = [middle[h, pl.ds(at, chunk), :] for h in range(2)]
        scale = scale_of(parts, start - reach1 + at)
        for h in range(2):
            normed[h, pl.ds(at, chunk), :] = parts[h] * scale * small[h, 1:2, :]
        return carry

    lax.fori_loop(0, lead // chunk, norm1, 0)
    convolve(1, mine, second)
    copies[2].wait()
    copies[3].wait()
    parts = []
    for h in range(2):
        cols = pl.ds(h * width, width)
        mixed = jnp.dot(act[0, 0:mine, :], weights[1, 0, :, cols], preferred_element_type=F32)
        mixed = mixed + jnp.dot(act[1, 0:mine, :], weights[1, 1, :, cols], preferred_element_type=F32)
        middle[h, pl.ds(reach1, mine), :] = middle[h, pl.ds(reach1, mine), :] + mixed
    hidden_own[...] = middle[own, pl.ds(reach1, mine), :]
    hidden_peer[...] = middle[other, pl.ds(reach1, mine), :]
    parts = [middle[h, pl.ds(reach1, mine), :] for h in range(2)]
    scale = scale_of(parts, None)
    for h in range(2):
        features[:, h * width : (h + 1) * width] = (parts[h] * scale * small[h, pl.ds(2 + 2 * taps, 1), :]).astype(BF16)


def project_kernel(place, own_ref, peer_ref, weight, out):
    count = own_ref.shape[0]
    at = pl.multiple_of(place[0] * count, count)
    back = pl.multiple_of((1 - place[0]) * count, count)
    out[pl.ds(at, count), :] = jnp.dot(own_ref[...], weight[...], preferred_element_type=F32).astype(BF16)
    out[pl.ds(back, count), :] = jnp.dot(peer_ref[...], weight[...], preferred_element_type=F32).astype(BF16)


def attend_kernel(*refs, count, scale, first, last):
    q_ref, blocks, refs = refs[0], refs[1 : 1 + count], refs[1 + count :]
    state_in, refs = ((), refs) if first else (refs[:2], refs[2:])
    factor = scale * math.log2(math.e)
    heads = q_ref.shape[1] // HD
    for head in range(heads):
        cols = slice(head * HD, (head + 1) * HD)
        q = q_ref[:, cols]
        scores = [
            lax.dot_general(kv[:, 0:HD], q, (((1,), (1,)), ((), ())), preferred_element_type=F32) for kv in blocks
        ]
        peaks = [jnp.max(s, axis=0, keepdims=True) for s in scores]
        total = None
        context = None
        if not first:
            stats, summed = state_in
            before = stats[head : head + 1, :]
            peaks.append(before)
        peak = functools.reduce(jnp.maximum, peaks)
        if not first:
            keep = jnp.exp2((before - peak) * factor)
            total = stats[heads + head : heads + head + 1, :] * keep
            context = summed[cols, :] * keep
        for s, kv in zip(scores, blocks):
            probs = jnp.exp2((s - peak) * factor)
            part = jnp.sum(probs, axis=0, keepdims=True)
            value = lax.dot_general(
                kv[:, HD:], probs.astype(BF16), (((0,), (0,)), ((), ())), preferred_element_type=F32
            )
            total = part if total is None else total + part
            context = value if context is None else context + value
        if last:
            refs[0][:, cols] = jnp.transpose(context * (1.0 / total)).astype(BF16)
        else:
            refs[0][head : head + 1, :] = peak
            refs[0][heads + head : heads + head + 1, :] = total
            refs[1][cols, :] = context


def begin_kernel(place, ctx, w_own, hid_own, hid_peer, out):
    count, width = hid_own.shape
    cols = pl.ds(pl.multiple_of(place[0] * width, 128), width)
    for at, hid in ((place[0] * count, hid_own), ((1 - place[0]) * count, hid_peer)):
        rows = pl.ds(pl.multiple_of(at, count), count)
        out[rows, :] = hid[...] + jnp.dot(ctx[rows, :], w_own[:, cols], preferred_element_type=F32)


def finish_kernel(place, ctx, w_peer, partial, out):
    width = partial.shape[1]
    cols = pl.ds(pl.multiple_of(place[0] * width, 128), width)
    mixed = jnp.dot(ctx[...], w_peer[:, cols], preferred_element_type=F32)
    out[...] = (partial[...] + mixed).astype(BF16)


def call(kernel, outs, name, mebibytes, *operands, specs=None, scratch=(), hbm_out=False):
    held, in_specs = [], []
    for i, operand in enumerate(operands):
        spec = (specs or {}).get(i, VMEM)
        in_specs.append(spec)
        space = pltpu.VMEM if spec is VMEM else pltpu.HBM if spec is ANY else None
        held.append(pltpu.with_memory_space_constraint(operand, space) if space else operand)
    shapes = tuple((jax.ShapeDtypeStruct if hbm_out else pltpu.VMEM)(shape, dtype) for shape, dtype in outs)
    result = pl.pallas_call(
        kernel,
        out_shape=shapes,
        in_specs=in_specs,
        out_specs=(VMEM,) * len(shapes),
        scratch_shapes=list(scratch),
        compiler_params=pltpu.CompilerParams(vmem_limit_bytes=mebibytes << 20),
        name=name,
    )(*held)
    return result if len(outs) > 1 else result[0]


def local(seq_in, conv_gain, dw_kernel, mix_weight, attn_gain, q_weight, kv_weight, out_weight):
    rows, width = seq_in.shape
    taps = dw_kernel.shape[1]
    size = lax.axis_size("seq")
    me = lax.axis_index("seq")
    core = lax.axis_index("ch")
    first, second = rows // 8, rows // 4
    reach1 = taps // 2 * second
    reach = taps // 2 * first + reach1
    mine = rows // 2
    lead = mine + 2 * reach1
    span = mine + 2 * reach

    even = me % 2 == 0
    low, high = seq_in[:reach], seq_in[rows - reach :]
    near_pairs = [(i, i ^ 1) for i in range(size)]
    far_pairs = [(0, 0), (size - 1, size - 1)]
    for i in range(1, size - 1, 2):
        far_pairs += [(i, i + 1), (i + 1, i)]
    to_near, to_far, x_sent, mix_sent, out_sent = lax.optimization_barrier(
        (jnp.where(even, high, low), jnp.where(even, low, high), seq_in, mix_weight, out_weight)
    )
    near = lax.ppermute(to_near, "seq", near_pairs)
    far = lax.ppermute(to_far, "seq", far_pairs)

    small = jnp.concatenate(
        [conv_gain, dw_kernel.reshape(2 * taps, width), attn_gain[None, :], jnp.zeros((3, width), F32)], axis=0
    )
    small_peer = peer(small)
    x_peer = peer(x_sent)
    mix_peer = peer(mix_sent)
    out_peer = peer(out_sent)
    bottom = rows + reach
    place = jnp.stack(
        [core, me * rows, jnp.where(even, bottom, 0), jnp.where(even, 0, bottom)]
    ).astype(jnp.int32)
    kv_flat = kv_weight.reshape(2 * width, 2 * kv_weight.shape[2])
    near, far, small, small_peer, x_peer, place, kv_flat = lax.optimization_barrier(
        (near, far, small, small_peer, x_peer, place, kv_flat)
    )
    near_peer = peer(near)
    far_peer = peer(far)

    features, hidden_own, hidden_away = call(
        functools.partial(
            tower_kernel, rows=rows, first=first, second=second, length=rows * size, taps=taps
        ),
        [((mine, 2 * width), BF16), ((mine, width), F32), ((mine, width), F32)],
        "tower",
        24,
        place, seq_in, x_peer, near, near_peer, far, far_peer, small, small_peer, mix_weight, mix_peer,
        specs={0: SMEM, 9: ANY, 10: ANY},
        scratch=[
            pltpu.VMEM((2, rows + 2 * reach, width), BF16),
            pltpu.VMEM((2, span, width), F32),
            pltpu.VMEM((2, lead, width), F32),
            pltpu.VMEM((2, lead, width), BF16),
            pltpu.VMEM((2,) + small.shape, F32),
            pltpu.VMEM((2, 2, width, 2 * width), BF16),
            pltpu.SemaphoreType.DMA((2, 2)),
        ],
    )

    features_peer = peer(features)

    def project(weight, name):
        return call(
            project_kernel, [((rows, weight.shape[1]), BF16)], name, 4, place, features, features_peer, weight,
            specs={0: SMEM},
        )

    kv = project(kv_flat, "keyvalue")
    order = ring_order(size)
    ahead = [(order[i], order[(i + 1) % size]) for i in range(size)]
    behind = [(b, a) for a, b in ahead]
    queries = None
    heads = q_weight.shape[1] // HD
    state = ()
    fresh = [kv]
    up = down = kv
    for step in range(size // 2):
        up = lax.ppermute(up, "seq", ahead)
        arrived = [up]
        if 2 * step + 2 < size:
            down = lax.ppermute(down, "seq", behind)
            arrived.append(down)
        if queries is None:
            queries = project(q_weight, "query")
            hidden_peer = peer(hidden_away)
        state = call(
            functools.partial(attend_kernel, count=len(fresh), scale=1.0 / math.sqrt(HD), first=step == 0, last=False),
            [((2 * heads, rows), F32), ((heads * HD, rows), F32)],
            "attend%d" % step,
            8,
            queries, *fresh, *state,
        )
        if step + 1 < size // 2:
            up, *state = lax.optimization_barrier((up, *state))
            if len(arrived) > 1:
                down, *state = lax.optimization_barrier((down, *state))
            arrived = [up, down]
        fresh = arrived
    context = call(
        functools.partial(attend_kernel, count=len(fresh), scale=1.0 / math.sqrt(HD), first=False, last=True),
        [((rows, heads * HD), BF16)],
        "attend_last",
        8,
        queries, *fresh, *state,
    )
    context_peer = peer(context)
    partial = call(
        begin_kernel, [((rows, width), F32)], "begin", 8, place, context, out_weight, hidden_own, hidden_peer, specs={0: SMEM}
    )
    return call(
        finish_kernel, [((rows, width), BF16)], "finish", 8, place, context_peer, out_peer, partial,
        specs={0: SMEM}, hbm_out=True,
    )


def solution(mesh):
    return jax.shard_map(
        local,
        mesh=mesh,
        in_specs=(
            P(("grp", "seq"), "ch"),
            P(None, "ch"),
            P(None, None, "ch"),
            P(None, "ch", None),
            P("ch"),
            P(None, "ch"),
            P(None, None, "ch"),
            P("ch", None),
        ),
        out_specs=P(("grp", "seq"), "ch"),
        check_vma=False,
    )
```

```python
import functools
import math

import jax
import jax.numpy as jnp
from jax import lax
from jax.experimental import pallas as pl
from jax.experimental.pallas import tpu as pltpu
from jax.sharding import PartitionSpec as P

HD = 128
EPSILON = 1e-06
BF16 = jnp.bfloat16
F32 = jnp.float32
SWAP = [(0, 1), (1, 0)]
VMEM = pl.BlockSpec(memory_space=pltpu.VMEM)
ANY = pl.BlockSpec(memory_space=pl.ANY)


def peer(array):
    return lax.ppermute(array, "ch", SWAP)


def ring_order(count):
    width = 1
    while width * width * 4 <= count:
        width *= 2
    rows = count // width
    if width == 1 or rows * width != count:
        return list(range(count))
    order = [row * width for row in range(rows)]
    for step, row in enumerate(reversed(range(rows))):
        columns = range(1, width) if step % 2 == 0 else range(width - 1, 0, -1)
        order += [row * width + column for column in columns]
    return order


def scale_of(parts, first_position, length):
    squares = jnp.sum(parts[0] * parts[0] + parts[1] * parts[1], axis=1, keepdims=True)
    scale = lax.rsqrt(squares / (2 * parts[0].shape[1]) + EPSILON)
    if first_position is None:
        return scale
    position = first_position + lax.broadcasted_iota(jnp.int32, scale.shape, 0)
    return jnp.where((position >= 0) & (position < length), scale, 0.0)


def convolve(normed, act, small, layer, begin, to, count, dilation, taps):
    block, strip, width = 32, 256, act.shape[2]

    def body(i, carry):
        at = pl.multiple_of(i * block, block)
        for h in range(2):
            for column in range(0, width, strip):
                cols = pl.ds(column, strip)
                total = None
                for tap in range(taps):
                    kernel = small[h, pl.ds(2 + layer * taps + tap, 1), cols]
                    term = normed[h, pl.ds(pl.multiple_of(begin + at + tap * dilation, 32), block), cols] * kernel
                    total = term if total is None else total + term
                act[h, pl.ds(pl.multiple_of(to + at, block), block), cols] = jax.nn.gelu(total, approximate=True).astype(BF16)
        return carry

    lax.fori_loop(0, count // block, body, 0)


def mix(act, weights, layer, count, half):
    width = act.shape[2]
    cols = pl.ds(half * width, width)
    mixed = jnp.dot(act[0, 0:count, :], weights[layer, 0, :, cols], preferred_element_type=F32)
    return mixed + jnp.dot(act[1, 0:count, :], weights[layer, 1, :, cols], preferred_element_type=F32)


CHUNK = 64


def inner_kernel(
    x_own, x_peer, small_own, small_peer, mix_own, mix_peer,
    small, normed, middle, middle_normed, weights,
    wide, act, sems,
    *, first, taps,
):
    own = lax.axis_index("ch")
    other = 1 - own
    rows, width = x_own.shape
    reach = taps // 2 * first
    count = rows - 2 * reach
    copies = []
    for layer in range(2):
        for side, source, at in ((own, mix_own, 0), (other, mix_peer, 1)):
            copies.append(pltpu.make_async_copy(source.at[layer], weights.at[layer, side], sems.at[layer, at]))
            copies[-1].start()
    small[own] = small_own[...]
    small[other] = small_peer[...]
    wide[own] = x_own[...]
    wide[other] = x_peer[...]

    def norm(i, carry):
        at = pl.multiple_of(i * CHUNK, CHUNK)
        parts = [wide[h, pl.ds(at, CHUNK), :].astype(F32) for h in range(2)]
        scale = scale_of(parts, None, None)
        for h in range(2):
            normed[h, pl.ds(at, CHUNK), :] = parts[h] * scale * small[h, 0:1, :]
        return carry

    lax.fori_loop(0, rows // CHUNK, norm, 0)
    convolve(normed, act, small, 0, 0, 0, count, first, taps)
    copies[0].wait()
    copies[1].wait()
    for h in range(2):
        middle[h] = wide[h, reach : reach + count, :].astype(F32) + mix(act, weights, 0, count, h)

    for at in range(0, count, CHUNK):
        parts = [middle[h, at : at + CHUNK, :] for h in range(2)]
        scale = scale_of(parts, None, None)
        for h in range(2):
            middle_normed[h, at : at + CHUNK, :] = parts[h] * scale * small[h, 1:2, :]
    copies[2].wait()
    copies[3].wait()


def tower_kernel(
    near_own, near_peer, far_own, far_peer, x_own, x_peer, small, inner, inner_middle, inner_normed, weights,
    features, hidden_own, hidden_peer,
    wide, normed, middle, act,
    *, first, second, length, taps,
):
    own = lax.axis_index("ch")
    other = 1 - own
    rows, width = x_own.shape
    first_reach = taps // 2 * first
    reach1 = taps // 2 * second
    reach = first_reach + reach1
    mine = rows // 2
    lead = mine + 2 * reach1
    done = rows - 2 * first_reach
    start = lax.axis_index("seq") * rows

    even = lax.axis_index("seq") % 2 == 0
    near_at = pl.multiple_of(jnp.where(even, rows + reach, 0), 64)
    far_at = pl.multiple_of(jnp.where(even, 0, rows + reach), 64)
    for side, body, near, far in ((own, x_own, near_own, far_own), (other, x_peer, near_peer, far_peer)):
        wide[side, pl.ds(reach, rows), :] = body[...]
        wide[side, pl.ds(near_at, reach), :] = near[...]
        wide[side, pl.ds(far_at, reach), :] = far[...]
    for h in range(2):
        normed[h, pl.ds(reach, rows), :] = inner[h]

    shift = own * mine
    above = reach - shift

    def norm0(i, carry):
        at = i * CHUNK
        at = pl.multiple_of(shift + jnp.where(at < above, at, at + rows), CHUNK)
        parts = [wide[h, pl.ds(at, CHUNK), :].astype(F32) for h in range(2)]
        scale = scale_of(parts, start - reach + at, length)
        for h in range(2):
            normed[h, pl.ds(at, CHUNK), :] = parts[h] * scale * small[h, 0:1, :]
        return carry

    lax.fori_loop(0, (mine + 2 * reach - rows) // CHUNK, norm0, 0)

    total = lead - done
    upper = reach1 + first_reach - shift
    block = 32

    def open_rows(i, carry):
        at = i * block
        source = pl.multiple_of(shift + jnp.where(at < upper, at, at + done), block)
        for h in range(2):
            for column in range(0, width, 256):
                cols = pl.ds(column, 256)
                total = None
                for tap in range(taps):
                    kernel = small[h, pl.ds(2 + tap, 1), cols]
                    term = normed[h, pl.ds(pl.multiple_of(source + tap * first, 32), block), cols] * kernel
                    total = term if total is None else total + term
                act[h, pl.ds(pl.multiple_of(at, block), block), cols] = jax.nn.gelu(total, approximate=True).astype(BF16)
        return carry

    lax.fori_loop(0, total // block, open_rows, 0)
    for h in range(2):
        mixed_rows = mix(act, weights, 0, total, h)
        middle[h, 0:total, :] = mixed_rows

    def norm1(i, carry):
        at = i * CHUNK
        to = pl.multiple_of(jnp.where(at < upper, at, at + done), CHUNK)
        here = pl.multiple_of(at, CHUNK)
        parts = []
        for h in range(2):
            before = wide[h, pl.ds(pl.multiple_of(shift + first_reach + to, 64), CHUNK), :].astype(F32)
            value = before + middle[h, pl.ds(here, CHUNK), :]
            middle[h, pl.ds(here, CHUNK), :] = value
            parts.append(value)
        scale = scale_of(parts, start + shift - reach1 + to, length)
        for h in range(2):
            normed[h, pl.ds(to, CHUNK), :] = parts[h] * scale * small[h, 1:2, :]
        return carry

    lax.fori_loop(0, total // CHUNK, norm1, 0)
    for h in range(2):
        normed[h, pl.ds(pl.multiple_of(upper, 64), done), :] = inner_normed[h]
    convolve(normed, act, small, 1, 0, 0, mine, second, taps)

    parts = []
    half = mine - first_reach
    for h in range(2):
        kept = inner_middle[h, pl.ds(pl.multiple_of(own * (done - half), 64), half), :]
        fresh = middle[h, pl.ds(pl.multiple_of((1 - own) * (upper - first_reach) + own * upper, 64), first_reach), :]
        mixed = mix(act, weights, 1, mine, h)
        low = jnp.where(own == 0, fresh, kept)
        high = jnp.where(own == 0, kept, fresh)
        parts.append(jnp.concatenate([low, high], axis=0) + mixed)
        middle[h, 0:mine, :] = parts[-1]
    hidden_own[...] = middle[own, 0:mine, :]
    hidden_peer[...] = middle[other, 0:mine, :]
    scale = scale_of(parts, None, None)
    for h in range(2):
        features[:, h * width : (h + 1) * width] = (parts[h] * scale * small[h, pl.ds(2 + 2 * taps, 1), :]).astype(BF16)


def project_kernel(own_ref, peer_ref, weight, out):
    count = own_ref.shape[0]
    own = lax.axis_index("ch")
    at = pl.multiple_of(own * count, count)
    back = pl.multiple_of((1 - own) * count, count)
    out[pl.ds(at, count), :] = jnp.dot(own_ref[...], weight[...], preferred_element_type=F32).astype(BF16)
    out[pl.ds(back, count), :] = jnp.dot(peer_ref[...], weight[...], preferred_element_type=F32).astype(BF16)


def attend_kernel(*refs, count, scale, first, last):
    q_ref, blocks, refs = refs[0], refs[1 : 1 + count], refs[1 + count :]
    state_in, refs = ((), refs) if first else (refs[:2], refs[2:])
    factor = scale * math.log2(math.e)
    heads = q_ref.shape[1] // HD
    for head in range(heads):
        cols = slice(head * HD, (head + 1) * HD)
        q = q_ref[:, cols]
        scores = [
            lax.dot_general(kv[:, 0:HD], q, (((1,), (1,)), ((), ())), preferred_element_type=F32) for kv in blocks
        ]
        peaks = [jnp.max(s, axis=0, keepdims=True) for s in scores]
        total = None
        context = None
        if not first:
            stats, summed = state_in
            before = stats[head : head + 1, :]
            peaks.append(before)
        peak = functools.reduce(jnp.maximum, peaks)
        if not first:
            keep = jnp.exp2((before - peak) * factor)
            total = stats[heads + head : heads + head + 1, :] * keep
            context = summed[cols, :] * keep
        for s, kv in zip(scores, blocks):
            probs = jnp.exp2((s - peak) * factor)
            part = jnp.sum(probs, axis=0, keepdims=True)
            value = lax.dot_general(
                kv[:, HD:], probs.astype(BF16), (((0,), (0,)), ((), ())), preferred_element_type=F32
            )
            total = part if total is None else total + part
            context = value if context is None else context + value
        if last:
            refs[0][:, cols] = jnp.transpose(context * (1.0 / total)).astype(BF16)
        else:
            refs[0][head : head + 1, :] = peak
            refs[0][heads + head : heads + head + 1, :] = total
            refs[1][cols, :] = context


def begin_kernel(ctx, w_own, hid_own, hid_peer, out):
    count, width = hid_own.shape
    own = lax.axis_index("ch")
    cols = pl.ds(pl.multiple_of(own * width, 128), width)
    for at, hid in ((own * count, hid_own), ((1 - own) * count, hid_peer)):
        rows = pl.ds(pl.multiple_of(at, count), count)
        out[rows, :] = hid[...] + jnp.dot(ctx[rows, :], w_own[:, cols], preferred_element_type=F32)


def finish_kernel(ctx, w_peer, partial, out, staged, sems):
    rows, width = partial.shape
    cols = pl.ds(pl.multiple_of(lax.axis_index("ch") * width, 128), width)
    copies = []
    count = rows // PIECES
    for piece in range(PIECES):
        here = pl.ds(piece * count, count)
        mixed = jnp.dot(ctx[here, :], w_peer[:, cols], preferred_element_type=F32)
        staged[here, :] = (partial[here, :] + mixed).astype(BF16)
        copies.append(pltpu.make_async_copy(staged.at[here, :], out.at[here, :], sems.at[piece]))
        copies[-1].start()
    for copy in copies:
        copy.wait()


def cut_kernel(x, to_near, to_far, sems):
    even = lax.axis_index("seq") % 2 == 0
    count = to_near.shape[0]
    last = x.shape[0] - count
    near = pltpu.make_async_copy(x.at[pl.ds(pl.multiple_of(jnp.where(even, last, 0), 64), count), :], to_near, sems.at[0])
    far = pltpu.make_async_copy(x.at[pl.ds(pl.multiple_of(jnp.where(even, 0, last), 64), count), :], to_far, sems.at[1])
    near.start()
    far.start()
    near.wait()
    far.wait()


PIECES = 2


def call(kernel, outs, name, mebibytes, *operands, hbm=(), scratch=(), hbm_out=False):
    held, in_specs = [], []
    for i, operand in enumerate(operands):
        in_specs.append(ANY if i in hbm else VMEM)
        held.append(pltpu.with_memory_space_constraint(operand, pltpu.HBM if i in hbm else pltpu.VMEM))
    shapes = tuple((pltpu.HBM if hbm_out else pltpu.VMEM)(shape, dtype) for shape, dtype in outs)
    result = pl.pallas_call(
        kernel,
        out_shape=shapes,
        in_specs=in_specs,
        out_specs=(ANY if hbm_out else VMEM,) * len(shapes),
        scratch_shapes=list(scratch),
        compiler_params=pltpu.CompilerParams(vmem_limit_bytes=mebibytes << 20),
        name=name,
    )(*held)
    return result if len(outs) > 1 else result[0]


def local(seq_in, conv_gain, dw_kernel, mix_weight, attn_gain, q_weight, kv_weight, out_weight):
    rows, width = seq_in.shape
    taps = dw_kernel.shape[1]
    size = lax.axis_size("seq")
    first, second = rows // 8, rows // 4
    first_reach = taps // 2 * first
    reach1 = taps // 2 * second
    reach = first_reach + reach1
    mine = rows // 2
    lead = mine + 2 * reach1
    done = rows - 2 * first_reach

    near_pairs = [(i, i ^ 1) for i in range(size)]
    far_pairs = [(0, 0), (size - 1, size - 1)]
    for i in range(1, size - 1, 2):
        far_pairs += [(i, i + 1), (i + 1, i)]
    to_near, to_far = call(
        cut_kernel, [((reach, width), BF16)] * 2, "cut", 2, seq_in, hbm=(0,), scratch=[pltpu.SemaphoreType.DMA((2,))]
    )
    to_near, to_far, x_sent, mix_sent, out_sent = lax.optimization_barrier(
        (to_near, to_far, seq_in, mix_weight, out_weight)
    )
    near = lax.ppermute(to_near, "seq", near_pairs)
    far = lax.ppermute(to_far, "seq", far_pairs)

    small = jnp.concatenate(
        [conv_gain, dw_kernel.reshape(2 * taps, width), attn_gain[None, :], jnp.zeros((3, width), F32)], axis=0
    )
    small_peer = peer(small)
    x_peer = peer(x_sent)
    mix_peer = peer(mix_sent)
    out_peer = peer(out_sent)
    kv_flat = kv_weight.reshape(2 * width, 2 * kv_weight.shape[2])

    inner = call(
        functools.partial(inner_kernel, first=first, taps=taps),
        [
            ((2,) + small.shape, F32),
            ((2, rows, width), F32),
            ((2, done, width), F32),
            ((2, done, width), F32),
            ((2, 2, width, 2 * width), BF16),
        ],
        "inner",
        4,
        seq_in, x_peer, small, small_peer, mix_weight, mix_peer,
        hbm=(4, 5),
        scratch=[
            pltpu.VMEM((2, rows, width), BF16),
            pltpu.VMEM((2, done, width), BF16),
            pltpu.SemaphoreType.DMA((2, 2)),
        ],
    )
    near, far, kv_flat, *inner = lax.optimization_barrier((near, far, kv_flat, *inner))
    near_peer = peer(near)
    far_peer = peer(far)

    features, hidden_own, hidden_away = call(
        functools.partial(tower_kernel, first=first, second=second, length=rows * size, taps=taps),
        [((mine, 2 * width), BF16), ((mine, width), F32), ((mine, width), F32)],
        "tower",
        12,
        near, near_peer, far, far_peer, seq_in, x_peer, *inner,
        scratch=[
            pltpu.VMEM((2, rows + 2 * reach, width), BF16),
            pltpu.VMEM((2, rows + 2 * reach, width), F32),
            pltpu.VMEM((2, lead - done, width), F32),
            pltpu.VMEM((2, lead - done, width), BF16),
        ],
    )

    features_peer = peer(features)

    def project(weight, name):
        return call(
            project_kernel, [((rows, weight.shape[1]), BF16)], name, 4, features, features_peer, weight
        )

    kv = project(kv_flat, "keyvalue")
    order = ring_order(size)
    ahead = [(order[i], order[(i + 1) % size]) for i in range(size)]
    behind = [(b, a) for a, b in ahead]
    queries = None
    heads = q_weight.shape[1] // HD
    state = ()
    fresh = [kv]
    up = down = kv
    for step in range(size // 2):
        up = lax.ppermute(up, "seq", ahead)
        arrived = [up]
        if 2 * step + 2 < size:
            down = lax.ppermute(down, "seq", behind)
            arrived.append(down)
        if queries is None:
            queries = project(q_weight, "query")
            hidden_peer = peer(hidden_away)
        state = call(
            functools.partial(attend_kernel, count=len(fresh), scale=1.0 / math.sqrt(HD), first=step == 0, last=False),
            [((2 * heads, rows), F32), ((heads * HD, rows), F32)],
            "attend%d" % step,
            8,
            queries, *fresh, *state,
        )
        if step + 1 < size // 2:
            up, *state = lax.optimization_barrier((up, *state))
            if len(arrived) > 1:
                down, *state = lax.optimization_barrier((down, *state))
            arrived = [up, down]
        fresh = arrived
    context = call(
        functools.partial(attend_kernel, count=len(fresh), scale=1.0 / math.sqrt(HD), first=False, last=True),
        [((rows, heads * HD), BF16)],
        "attend_last",
        8,
        queries, *fresh, *state,
    )
    context_peer = peer(context)
    partial = call(
        begin_kernel, [((rows, width), F32)], "begin", 4, context, out_weight, hidden_own, hidden_peer
    )
    return call(
        finish_kernel, [((rows, width), BF16)], "finish", 4, context_peer, out_peer, partial,
        scratch=[pltpu.VMEM((rows, width), BF16), pltpu.SemaphoreType.DMA((PIECES,))], hbm_out=True,
    )


def solution(mesh):
    return jax.shard_map(
        local,
        mesh=mesh,
        in_specs=(
            P(("grp", "seq"), "ch"),
            P(None, "ch"),
            P(None, None, "ch"),
            P(None, "ch", None),
            P("ch"),
            P(None, "ch"),
            P(None, None, "ch"),
            P("ch", None),
        ),
        out_specs=P(("grp", "seq"), "ch"),
        check_vma=False,
    )
```

```python
import functools
import math

import jax
import jax.numpy as jnp
from jax import lax
from jax.experimental import pallas as pl
from jax.experimental.pallas import tpu as pltpu
from jax.sharding import PartitionSpec as P

HD = 128
EPSILON = 1e-06
BF16 = jnp.bfloat16
F32 = jnp.float32
SWAP = [(0, 1), (1, 0)]
VMEM = pl.BlockSpec(memory_space=pltpu.VMEM)
ANY = pl.BlockSpec(memory_space=pl.ANY)


def peer(array):
    return lax.ppermute(array, "ch", SWAP)


def ring_order(count):
    width = 1
    while width * width * 4 <= count:
        width *= 2
    rows = count // width
    if width == 1 or rows * width != count:
        return list(range(count))
    order = [row * width for row in range(rows)]
    for step, row in enumerate(reversed(range(rows))):
        columns = range(1, width) if step % 2 == 0 else range(width - 1, 0, -1)
        order += [row * width + column for column in columns]
    return order


def scale_of(parts, first_position, length):
    squares = jnp.sum(parts[0] * parts[0] + parts[1] * parts[1], axis=1, keepdims=True)
    scale = lax.rsqrt(squares / (2 * parts[0].shape[1]) + EPSILON)
    if first_position is None:
        return scale
    position = first_position + lax.broadcasted_iota(jnp.int32, scale.shape, 0)
    return jnp.where((position >= 0) & (position < length), scale, 0.0)


def convolve(normed, act, small, layer, begin, to, count, dilation, taps):
    block, strip, width = 32, 256, act.shape[2]

    def body(i, carry):
        at = pl.multiple_of(i * block, block)
        for h in range(2):
            for column in range(0, width, strip):
                cols = pl.ds(column, strip)
                total = None
                for tap in range(taps):
                    kernel = small[h, pl.ds(2 + layer * taps + tap, 1), cols]
                    term = normed[h, pl.ds(pl.multiple_of(begin + at + tap * dilation, 32), block), cols] * kernel
                    total = term if total is None else total + term
                act[h, pl.ds(pl.multiple_of(to + at, block), block), cols] = jax.nn.gelu(total, approximate=True).astype(BF16)
        return carry

    lax.fori_loop(0, count // block, body, 0)


def mix(act, weights, layer, count, half):
    width = act.shape[2]
    cols = pl.ds(half * width, width)
    mixed = jnp.dot(act[0, 0:count, :], weights[layer, 0, :, cols], preferred_element_type=F32)
    return mixed + jnp.dot(act[1, 0:count, :], weights[layer, 1, :, cols], preferred_element_type=F32)


CHUNK = 64


def inner_kernel(
    x_own, x_peer, small_own, small_peer, mix_own, mix_peer,
    small, normed, middle, middle_normed, weights,
    wide, act, sems,
    *, first, taps,
):
    own = lax.axis_index("ch")
    other = 1 - own
    rows, width = x_own.shape
    reach = taps // 2 * first
    count = rows - 2 * reach
    copies = []
    for layer in range(2):
        for side, source, at in ((own, mix_own, 0), (other, mix_peer, 1)):
            copies.append(pltpu.make_async_copy(source.at[layer], weights.at[layer, side], sems.at[layer, at]))
            copies[-1].start()
    small[own] = small_own[...]
    small[other] = small_peer[...]
    wide[own] = x_own[...]
    wide[other] = x_peer[...]

    def norm(i, carry):
        at = pl.multiple_of(i * CHUNK, CHUNK)
        parts = [wide[h, pl.ds(at, CHUNK), :].astype(F32) for h in range(2)]
        scale = scale_of(parts, None, None)
        for h in range(2):
            normed[h, pl.ds(at, CHUNK), :] = parts[h] * scale * small[h, 0:1, :]
        return carry

    lax.fori_loop(0, rows // CHUNK, norm, 0)
    convolve(normed, act, small, 0, 0, 0, count, first, taps)
    copies[0].wait()
    copies[1].wait()
    for h in range(2):
        middle[h] = wide[h, reach : reach + count, :].astype(F32) + mix(act, weights, 0, count, h)

    for at in range(0, count, CHUNK):
        parts = [middle[h, at : at + CHUNK, :] for h in range(2)]
        scale = scale_of(parts, None, None)
        for h in range(2):
            middle_normed[h, at : at + CHUNK, :] = parts[h] * scale * small[h, 1:2, :]
    copies[2].wait()
    copies[3].wait()


def tower_kernel(
    near_own, near_peer, far_own, far_peer, x_own, x_peer, small, inner, inner_middle, inner_normed, weights,
    features, hidden_own, hidden_peer,
    wide, normed, middle, act,
    *, first, second, length, taps,
):
    own = lax.axis_index("ch")
    other = 1 - own
    rows, width = x_own.shape
    first_reach = taps // 2 * first
    reach1 = taps // 2 * second
    reach = first_reach + reach1
    mine = rows // 2
    lead = mine + 2 * reach1
    done = rows - 2 * first_reach
    start = lax.axis_index("seq") * rows

    even = lax.axis_index("seq") % 2 == 0
    near_at = pl.multiple_of(jnp.where(even, rows + reach, 0), 64)
    far_at = pl.multiple_of(jnp.where(even, 0, rows + reach), 64)
    for side, body, near, far in ((own, x_own, near_own, far_own), (other, x_peer, near_peer, far_peer)):
        wide[side, pl.ds(reach, rows), :] = body[...]
        wide[side, pl.ds(near_at, reach), :] = near[...]
        wide[side, pl.ds(far_at, reach), :] = far[...]
    for h in range(2):
        normed[h, pl.ds(reach, rows), :] = inner[h]

    shift = own * mine
    above = reach - shift

    def norm0(i, carry):
        at = i * CHUNK
        at = pl.multiple_of(shift + jnp.where(at < above, at, at + rows), CHUNK)
        parts = [wide[h, pl.ds(at, CHUNK), :].astype(F32) for h in range(2)]
        scale = scale_of(parts, start - reach + at, length)
        for h in range(2):
            normed[h, pl.ds(at, CHUNK), :] = parts[h] * scale * small[h, 0:1, :]
        return carry

    lax.fori_loop(0, (mine + 2 * reach - rows) // CHUNK, norm0, 0)

    total = lead - done
    upper = reach1 + first_reach - shift
    block = 32

    def open_rows(i, carry):
        at = i * block
        source = pl.multiple_of(shift + jnp.where(at < upper, at, at + done), block)
        for h in range(2):
            for column in range(0, width, 256):
                cols = pl.ds(column, 256)
                total = None
                for tap in range(taps):
                    kernel = small[h, pl.ds(2 + tap, 1), cols]
                    term = normed[h, pl.ds(pl.multiple_of(source + tap * first, 32), block), cols] * kernel
                    total = term if total is None else total + term
                act[h, pl.ds(pl.multiple_of(at, block), block), cols] = jax.nn.gelu(total, approximate=True).astype(BF16)
        return carry

    lax.fori_loop(0, total // block, open_rows, 0)
    for h in range(2):
        mixed_rows = mix(act, weights, 0, total, h)
        middle[h, 0:total, :] = mixed_rows

    def norm1(i, carry):
        at = i * CHUNK
        to = pl.multiple_of(jnp.where(at < upper, at, at + done), CHUNK)
        here = pl.multiple_of(at, CHUNK)
        parts = []
        for h in range(2):
            before = wide[h, pl.ds(pl.multiple_of(shift + first_reach + to, 64), CHUNK), :].astype(F32)
            value = before + middle[h, pl.ds(here, CHUNK), :]
            middle[h, pl.ds(here, CHUNK), :] = value
            parts.append(value)
        scale = scale_of(parts, start + shift - reach1 + to, length)
        for h in range(2):
            normed[h, pl.ds(to, CHUNK), :] = parts[h] * scale * small[h, 1:2, :]
        return carry

    lax.fori_loop(0, total // CHUNK, norm1, 0)
    for h in range(2):
        normed[h, pl.ds(pl.multiple_of(upper, 64), done), :] = inner_normed[h]
    convolve(normed, act, small, 1, 0, 0, mine, second, taps)

    parts = []
    half = mine - first_reach
    for h in range(2):
        kept = inner_middle[h, pl.ds(pl.multiple_of(own * (done - half), 64), half), :]
        fresh = middle[h, pl.ds(pl.multiple_of((1 - own) * (upper - first_reach) + own * upper, 64), first_reach), :]
        mixed = mix(act, weights, 1, mine, h)
        low = jnp.where(own == 0, fresh, kept)
        high = jnp.where(own == 0, kept, fresh)
        parts.append(jnp.concatenate([low, high], axis=0) + mixed)
        middle[h, 0:mine, :] = parts[-1]
    hidden_own[...] = middle[own, 0:mine, :]
    hidden_peer[...] = middle[other, 0:mine, :]
    scale = scale_of(parts, None, None)
    for h in range(2):
        features[:, h * width : (h + 1) * width] = (parts[h] * scale * small[h, pl.ds(2 + 2 * taps, 1), :]).astype(BF16)


def project_kernel(own_ref, peer_ref, weight, out):
    count = own_ref.shape[0]
    own = lax.axis_index("ch")
    at = pl.multiple_of(own * count, count)
    back = pl.multiple_of((1 - own) * count, count)
    out[pl.ds(at, count), :] = jnp.dot(own_ref[...], weight[...], preferred_element_type=F32).astype(BF16)
    out[pl.ds(back, count), :] = jnp.dot(peer_ref[...], weight[...], preferred_element_type=F32).astype(BF16)


def halve_kernel(ahead, behind, upper, lower):
    count = upper.shape[0]
    upper[...] = ahead[0:count, :]
    lower[...] = behind[count:, :]


def attend_kernel(*refs, count, scale, first, last):
    q_ref, blocks, refs = refs[0], refs[1 : 1 + count], refs[1 + count :]
    state_in, refs = ((), refs) if first else (refs[:2], refs[2:])
    factor = scale * math.log2(math.e)
    heads = q_ref.shape[1] // HD
    for head in range(heads):
        cols = slice(head * HD, (head + 1) * HD)
        q = q_ref[:, cols]
        scores = [
            lax.dot_general(kv[:, 0:HD], q, (((1,), (1,)), ((), ())), preferred_element_type=F32) for kv in blocks
        ]
        peaks = [jnp.max(s, axis=0, keepdims=True) for s in scores]
        total = None
        context = None
        if not first:
            stats, summed = state_in
            before = stats[head : head + 1, :]
            peaks.append(before)
        peak = functools.reduce(jnp.maximum, peaks)
        if not first:
            keep = jnp.exp2((before - peak) * factor)
            total = stats[heads + head : heads + head + 1, :] * keep
            context = summed[cols, :] * keep
        for s, kv in zip(scores, blocks):
            probs = jnp.exp2((s - peak) * factor)
            part = jnp.sum(probs, axis=0, keepdims=True)
            value = lax.dot_general(
                kv[:, HD:], probs.astype(BF16), (((0,), (0,)), ((), ())), preferred_element_type=F32
            )
            total = part if total is None else total + part
            context = value if context is None else context + value
        if last:
            refs[0][:, cols] = jnp.transpose(context * (1.0 / total)).astype(BF16)
        else:
            refs[0][head : head + 1, :] = peak
            refs[0][heads + head : heads + head + 1, :] = total
            refs[1][cols, :] = context


def begin_kernel(ctx, w_own, hid_own, hid_peer, out):
    count, width = hid_own.shape
    own = lax.axis_index("ch")
    cols = pl.ds(pl.multiple_of(own * width, 128), width)
    for at, hid in ((own * count, hid_own), ((1 - own) * count, hid_peer)):
        rows = pl.ds(pl.multiple_of(at, count), count)
        out[rows, :] = hid[...] + jnp.dot(ctx[rows, :], w_own[:, cols], preferred_element_type=F32)


def finish_kernel(ctx, w_peer, partial, out, staged, sems):
    rows, width = partial.shape
    cols = pl.ds(pl.multiple_of(lax.axis_index("ch") * width, 128), width)
    copies = []
    count = rows // PIECES
    for piece in range(PIECES):
        here = pl.ds(piece * count, count)
        mixed = jnp.dot(ctx[here, :], w_peer[:, cols], preferred_element_type=F32)
        staged[here, :] = (partial[here, :] + mixed).astype(BF16)
        copies.append(pltpu.make_async_copy(staged.at[here, :], out.at[here, :], sems.at[piece]))
        copies[-1].start()
    for copy in copies:
        copy.wait()


def cut_kernel(x, to_near, to_far, sems):
    even = lax.axis_index("seq") % 2 == 0
    count = to_near.shape[0]
    last = x.shape[0] - count
    near = pltpu.make_async_copy(x.at[pl.ds(pl.multiple_of(jnp.where(even, last, 0), 64), count), :], to_near, sems.at[0])
    far = pltpu.make_async_copy(x.at[pl.ds(pl.multiple_of(jnp.where(even, 0, last), 64), count), :], to_far, sems.at[1])
    near.start()
    far.start()
    near.wait()
    far.wait()


PIECES = 2


def call(kernel, outs, name, mebibytes, *operands, hbm=(), scratch=(), hbm_out=False):
    held, in_specs = [], []
    for i, operand in enumerate(operands):
        in_specs.append(ANY if i in hbm else VMEM)
        held.append(pltpu.with_memory_space_constraint(operand, pltpu.HBM if i in hbm else pltpu.VMEM))
    shapes = tuple((pltpu.HBM if hbm_out else pltpu.VMEM)(shape, dtype) for shape, dtype in outs)
    result = pl.pallas_call(
        kernel,
        out_shape=shapes,
        in_specs=in_specs,
        out_specs=(ANY if hbm_out else VMEM,) * len(shapes),
        scratch_shapes=list(scratch),
        compiler_params=pltpu.CompilerParams(vmem_limit_bytes=mebibytes << 20),
        name=name,
    )(*held)
    return result if len(outs) > 1 else result[0]


def local(seq_in, conv_gain, dw_kernel, mix_weight, attn_gain, q_weight, kv_weight, out_weight):
    rows, width = seq_in.shape
    taps = dw_kernel.shape[1]
    size = lax.axis_size("seq")
    first, second = rows // 8, rows // 4
    first_reach = taps // 2 * first
    reach1 = taps // 2 * second
    reach = first_reach + reach1
    mine = rows // 2
    lead = mine + 2 * reach1
    done = rows - 2 * first_reach

    near_pairs = [(i, i ^ 1) for i in range(size)]
    far_pairs = [(0, 0), (size - 1, size - 1)]
    for i in range(1, size - 1, 2):
        far_pairs += [(i, i + 1), (i + 1, i)]
    to_near, to_far = call(
        cut_kernel, [((reach, width), BF16)] * 2, "cut", 2, seq_in, hbm=(0,), scratch=[pltpu.SemaphoreType.DMA((2,))]
    )
    to_near, to_far, x_sent, mix_sent, out_sent = lax.optimization_barrier(
        (to_near, to_far, seq_in, mix_weight, out_weight)
    )
    near = lax.ppermute(to_near, "seq", near_pairs)
    far = lax.ppermute(to_far, "seq", far_pairs)

    small = jnp.concatenate(
        [conv_gain, dw_kernel.reshape(2 * taps, width), attn_gain[None, :], jnp.zeros((3, width), F32)], axis=0
    )
    small_peer = peer(small)
    x_peer = peer(x_sent)
    mix_peer = peer(mix_sent)
    out_peer = peer(out_sent)
    kv_flat = kv_weight.reshape(2 * width, 2 * kv_weight.shape[2])

    inner = call(
        functools.partial(inner_kernel, first=first, taps=taps),
        [
            ((2,) + small.shape, F32),
            ((2, rows, width), F32),
            ((2, done, width), F32),
            ((2, done, width), F32),
            ((2, 2, width, 2 * width), BF16),
        ],
        "inner",
        4,
        seq_in, x_peer, small, small_peer, mix_weight, mix_peer,
        hbm=(4, 5),
        scratch=[
            pltpu.VMEM((2, rows, width), BF16),
            pltpu.VMEM((2, done, width), BF16),
            pltpu.SemaphoreType.DMA((2, 2)),
        ],
    )
    near, far, kv_flat, *inner = lax.optimization_barrier((near, far, kv_flat, *inner))
    near_peer = peer(near)
    far_peer = peer(far)

    features, hidden_own, hidden_away = call(
        functools.partial(tower_kernel, first=first, second=second, length=rows * size, taps=taps),
        [((mine, 2 * width), BF16), ((mine, width), F32), ((mine, width), F32)],
        "tower",
        12,
        near, near_peer, far, far_peer, seq_in, x_peer, *inner,
        scratch=[
            pltpu.VMEM((2, rows + 2 * reach, width), BF16),
            pltpu.VMEM((2, rows + 2 * reach, width), F32),
            pltpu.VMEM((2, lead - done, width), F32),
            pltpu.VMEM((2, lead - done, width), BF16),
        ],
    )

    features_peer = peer(features)

    def project(weight, name):
        return call(
            project_kernel, [((rows, weight.shape[1]), BF16)], name, 4, features, features_peer, weight
        )

    kv = project(kv_flat, "keyvalue")
    order = ring_order(size)
    ahead = [(order[i], order[(i + 1) % size]) for i in range(size)]
    behind = [(b, a) for a, b in ahead]
    queries = None
    heads = q_weight.shape[1] // HD
    skip = [(order[i], order[(i + 2) % size]) for i in range(size)]
    skip_back = [(b, a) for a, b in skip]
    attend = functools.partial(attend_kernel, scale=1.0 / math.sqrt(HD))
    hidden_peer = peer(hidden_away)
    state, fresh = (), [kv]
    up = down = kv
    laps = size // 2 - 1
    for step in range(laps + 1):
        if step < laps:
            ahead_of, behind_of = up, down
            up = lax.ppermute(ahead_of, "seq", ahead)
            down = lax.ppermute(behind_of, "seq", behind)
            if step == laps - 1:
                halves = call(halve_kernel, [((rows // 2, kv.shape[1]), BF16)] * 2, "halve", 2, ahead_of, behind_of)
                opposite = [lax.ppermute(halves[0], "seq", skip), lax.ppermute(halves[1], "seq", skip_back)]
        if queries is None:
            queries = project(q_weight, "query")
        state = call(
            functools.partial(attend, count=len(fresh), first=step == 0, last=False),
            [((2 * heads, rows), F32), ((heads * HD, rows), F32)],
            "attend%d" % step,
            8,
            queries, *fresh, *state,
        )
        if step < laps:
            up, *state = lax.optimization_barrier((up, *state))
            down, *state = lax.optimization_barrier((down, *state))
            fresh = [up, down]
    context = call(
        functools.partial(attend, count=len(opposite), first=False, last=True),
        [((rows, heads * HD), BF16)],
        "attend_last",
        8,
        queries, *opposite, *state,
    )
    context_peer = peer(context)
    partial = call(
        begin_kernel, [((rows, width), F32)], "begin", 4, context, out_weight, hidden_own, hidden_peer
    )
    return call(
        finish_kernel, [((rows, width), BF16)], "finish", 4, context_peer, out_peer, partial,
        scratch=[pltpu.VMEM((rows, width), BF16), pltpu.SemaphoreType.DMA((PIECES,))], hbm_out=True,
    )


def solution(mesh):
    return jax.shard_map(
        local,
        mesh=mesh,
        in_specs=(
            P(("grp", "seq"), "ch"),
            P(None, "ch"),
            P(None, None, "ch"),
            P(None, "ch", None),
            P("ch"),
            P(None, "ch"),
            P(None, None, "ch"),
            P("ch", None),
        ),
        out_specs=P(("grp", "seq"), "ch"),
        check_vma=False,
    )
```

```python
import functools
import math

import jax
import jax.numpy as jnp
from jax import lax
from jax.experimental import pallas as pl
from jax.experimental.pallas import tpu as pltpu
from jax.sharding import PartitionSpec as P

HD = 128
EPSILON = 1e-06
BF16 = jnp.bfloat16
F32 = jnp.float32
SWAP = [(0, 1), (1, 0)]
VMEM = pl.BlockSpec(memory_space=pltpu.VMEM)
ANY = pl.BlockSpec(memory_space=pl.ANY)


def peer(array):
    return lax.ppermute(array, "ch", SWAP)


def ring_order(count):
    width = 1
    while width * width * 4 <= count:
        width *= 2
    rows = count // width
    if width == 1 or rows * width != count:
        return list(range(count))
    order = [row * width for row in range(rows)]
    for step, row in enumerate(reversed(range(rows))):
        columns = range(1, width) if step % 2 == 0 else range(width - 1, 0, -1)
        order += [row * width + column for column in columns]
    return order


def scale_of(parts, first_position, length):
    squares = jnp.sum(parts[0] * parts[0] + parts[1] * parts[1], axis=1, keepdims=True)
    scale = lax.rsqrt(squares / (2 * parts[0].shape[1]) + EPSILON)
    if first_position is None:
        return scale
    position = first_position + lax.broadcasted_iota(jnp.int32, scale.shape, 0)
    return jnp.where((position >= 0) & (position < length), scale, 0.0)


def convolve(normed, act, small, layer, begin, to, count, dilation, taps):
    block, strip, width = 32, 256, act.shape[2]

    def body(i, carry):
        at = pl.multiple_of(i * block, block)
        for h in range(2):
            for column in range(0, width, strip):
                cols = pl.ds(column, strip)
                total = None
                for tap in range(taps):
                    kernel = small[h, pl.ds(2 + layer * taps + tap, 1), cols]
                    term = normed[h, pl.ds(pl.multiple_of(begin + at + tap * dilation, 32), block), cols] * kernel
                    total = term if total is None else total + term
                act[h, pl.ds(pl.multiple_of(to + at, block), block), cols] = jax.nn.gelu(total, approximate=True).astype(BF16)
        return carry

    lax.fori_loop(0, count // block, body, 0)


def mix(act, weights, layer, count, half):
    width = act.shape[2]
    cols = pl.ds(half * width, width)
    mixed = jnp.dot(act[0, 0:count, :], weights[layer, 0, :, cols], preferred_element_type=F32)
    return mixed + jnp.dot(act[1, 0:count, :], weights[layer, 1, :, cols], preferred_element_type=F32)


CHUNK = 64


def inner_kernel(
    x_own, x_peer, small_own, small_peer, mix_own, mix_peer,
    small, normed, middle, middle_normed, weights,
    wide, act, sems,
    *, first, taps,
):
    own = lax.axis_index("ch")
    other = 1 - own
    rows, width = x_own.shape
    reach = taps // 2 * first
    count = rows - 2 * reach
    copies = []
    for layer in range(2):
        for side, source, at in ((own, mix_own, 0), (other, mix_peer, 1)):
            copies.append(pltpu.make_async_copy(source.at[layer], weights.at[layer, side], sems.at[layer, at]))
            copies[-1].start()
    small[own] = small_own[...]
    small[other] = small_peer[...]
    wide[own] = x_own[...]
    wide[other] = x_peer[...]

    def norm(i, carry):
        at = pl.multiple_of(i * CHUNK, CHUNK)
        parts = [wide[h, pl.ds(at, CHUNK), :].astype(F32) for h in range(2)]
        scale = scale_of(parts, None, None)
        for h in range(2):
            normed[h, pl.ds(at, CHUNK), :] = parts[h] * scale * small[h, 0:1, :]
        return carry

    lax.fori_loop(0, rows // CHUNK, norm, 0)
    convolve(normed, act, small, 0, 0, 0, count, first, taps)
    copies[0].wait()
    copies[1].wait()
    for h in range(2):
        middle[h] = wide[h, reach : reach + count, :].astype(F32) + mix(act, weights, 0, count, h)

    for at in range(0, count, CHUNK):
        parts = [middle[h, at : at + CHUNK, :] for h in range(2)]
        scale = scale_of(parts, None, None)
        for h in range(2):
            middle_normed[h, at : at + CHUNK, :] = parts[h] * scale * small[h, 1:2, :]
    copies[2].wait()
    copies[3].wait()


def tower_kernel(
    near_own, near_peer, far_own, far_peer, x_own, x_peer, small, inner, inner_middle, inner_normed, weights,
    features, hidden_own, hidden_peer,
    wide, normed, middle, act,
    *, first, second, length, taps,
):
    own = lax.axis_index("ch")
    other = 1 - own
    rows, width = x_own.shape
    first_reach = taps // 2 * first
    reach1 = taps // 2 * second
    reach = first_reach + reach1
    mine = rows // 2
    lead = mine + 2 * reach1
    done = rows - 2 * first_reach
    start = lax.axis_index("seq") * rows

    even = lax.axis_index("seq") % 2 == 0
    near_at = pl.multiple_of(jnp.where(even, rows + reach, 0), 64)
    far_at = pl.multiple_of(jnp.where(even, 0, rows + reach), 64)
    for side, body, near, far in ((own, x_own, near_own, far_own), (other, x_peer, near_peer, far_peer)):
        wide[side, pl.ds(reach, rows), :] = body[...]
        wide[side, pl.ds(near_at, reach), :] = near[...]
        wide[side, pl.ds(far_at, reach), :] = far[...]
    for h in range(2):
        normed[h, pl.ds(reach, rows), :] = inner[h]

    shift = own * mine
    above = reach - shift

    def norm0(i, carry):
        at = i * CHUNK
        at = pl.multiple_of(shift + jnp.where(at < above, at, at + rows), CHUNK)
        parts = [wide[h, pl.ds(at, CHUNK), :].astype(F32) for h in range(2)]
        scale = scale_of(parts, start - reach + at, length)
        for h in range(2):
            normed[h, pl.ds(at, CHUNK), :] = parts[h] * scale * small[h, 0:1, :]
        return carry

    lax.fori_loop(0, (mine + 2 * reach - rows) // CHUNK, norm0, 0)

    total = lead - done
    upper = reach1 + first_reach - shift
    block = 32

    def open_rows(i, carry):
        at = i * block
        source = pl.multiple_of(shift + jnp.where(at < upper, at, at + done), block)
        for h in range(2):
            for column in range(0, width, 256):
                cols = pl.ds(column, 256)
                total = None
                for tap in range(taps):
                    kernel = small[h, pl.ds(2 + tap, 1), cols]
                    term = normed[h, pl.ds(pl.multiple_of(source + tap * first, 32), block), cols] * kernel
                    total = term if total is None else total + term
                act[h, pl.ds(pl.multiple_of(at, block), block), cols] = jax.nn.gelu(total, approximate=True).astype(BF16)
        return carry

    lax.fori_loop(0, total // block, open_rows, 0)
    for h in range(2):
        mixed_rows = mix(act, weights, 0, total, h)
        middle[h, 0:total, :] = mixed_rows

    def norm1(i, carry):
        at = i * CHUNK
        to = pl.multiple_of(jnp.where(at < upper, at, at + done), CHUNK)
        here = pl.multiple_of(at, CHUNK)
        parts = []
        for h in range(2):
            before = wide[h, pl.ds(pl.multiple_of(shift + first_reach + to, 64), CHUNK), :].astype(F32)
            value = before + middle[h, pl.ds(here, CHUNK), :]
            middle[h, pl.ds(here, CHUNK), :] = value
            parts.append(value)
        scale = scale_of(parts, start + shift - reach1 + to, length)
        for h in range(2):
            normed[h, pl.ds(to, CHUNK), :] = parts[h] * scale * small[h, 1:2, :]
        return carry

    lax.fori_loop(0, total // CHUNK, norm1, 0)
    for h in range(2):
        normed[h, pl.ds(pl.multiple_of(upper, 64), done), :] = inner_normed[h]
    convolve(normed, act, small, 1, 0, 0, mine, second, taps)

    parts = []
    half = mine - first_reach
    for h in range(2):
        kept = inner_middle[h, pl.ds(pl.multiple_of(own * (done - half), 64), half), :]
        fresh = middle[h, pl.ds(pl.multiple_of((1 - own) * (upper - first_reach) + own * upper, 64), first_reach), :]
        mixed = mix(act, weights, 1, mine, h)
        low = jnp.where(own == 0, fresh, kept)
        high = jnp.where(own == 0, kept, fresh)
        parts.append(jnp.concatenate([low, high], axis=0) + mixed)
        middle[h, 0:mine, :] = parts[-1]
    hidden_own[...] = middle[own, 0:mine, :]
    hidden_peer[...] = middle[other, 0:mine, :]
    scale = scale_of(parts, None, None)
    for h in range(2):
        features[:, h * width : (h + 1) * width] = (parts[h] * scale * small[h, pl.ds(2 + 2 * taps, 1), :]).astype(BF16)


def project_kernel(own_ref, peer_ref, weight, out):
    count = own_ref.shape[0]
    own = lax.axis_index("ch")
    at = pl.multiple_of(own * count, count)
    back = pl.multiple_of((1 - own) * count, count)
    out[pl.ds(at, count), :] = jnp.dot(own_ref[...], weight[...], preferred_element_type=F32).astype(BF16)
    out[pl.ds(back, count), :] = jnp.dot(peer_ref[...], weight[...], preferred_element_type=F32).astype(BF16)


def halve_kernel(ahead, behind, upper, lower):
    count = upper.shape[0]
    upper[...] = ahead[0:count, :]
    lower[...] = behind[count:, :]


def attend_kernel(*refs, count, scale, first, last):
    q_ref, blocks, refs = refs[0], refs[1 : 1 + count], refs[1 + count :]
    state_in, refs = ((), refs) if first else (refs[:2], refs[2:])
    factor = scale * math.log2(math.e)
    heads = q_ref.shape[1] // HD
    for head in range(heads):
        cols = slice(head * HD, (head + 1) * HD)
        q = q_ref[:, cols]
        scores = [
            lax.dot_general(kv[:, 0:HD], q, (((1,), (1,)), ((), ())), preferred_element_type=F32) for kv in blocks
        ]
        peaks = [jnp.max(s, axis=0, keepdims=True) for s in scores]
        total = None
        context = None
        if not first:
            stats, summed = state_in
            before = stats[head : head + 1, :]
            peaks.append(before)
        peak = functools.reduce(jnp.maximum, peaks)
        if not first:
            keep = jnp.exp2((before - peak) * factor)
            total = stats[heads + head : heads + head + 1, :] * keep
            context = summed[cols, :] * keep
        for s, kv in zip(scores, blocks):
            probs = jnp.exp2((s - peak) * factor)
            part = jnp.sum(probs, axis=0, keepdims=True)
            value = lax.dot_general(
                kv[:, HD:], probs.astype(BF16), (((0,), (0,)), ((), ())), preferred_element_type=F32
            )
            total = part if total is None else total + part
            context = value if context is None else context + value
        if last:
            refs[0][:, cols] = jnp.transpose(context * (1.0 / total)).astype(BF16)
        else:
            refs[0][head : head + 1, :] = peak
            refs[0][heads + head : heads + head + 1, :] = total
            refs[1][cols, :] = context


def begin_kernel(ctx, w_own, hid_own, hid_peer, out):
    count, width = hid_own.shape
    own = lax.axis_index("ch")
    cols = pl.ds(pl.multiple_of(own * width, 128), width)
    for at, hid in ((own * count, hid_own), ((1 - own) * count, hid_peer)):
        rows = pl.ds(pl.multiple_of(at, count), count)
        out[rows, :] = hid[...] + jnp.dot(ctx[rows, :], w_own[:, cols], preferred_element_type=F32)


def finish_kernel(ctx, w_peer, partial, out, staged, sems):
    rows, width = partial.shape
    cols = pl.ds(pl.multiple_of(lax.axis_index("ch") * width, 128), width)
    copies = []
    count = rows // PIECES
    for piece in range(PIECES):
        here = pl.ds(piece * count, count)
        mixed = jnp.dot(ctx[here, :], w_peer[:, cols], preferred_element_type=F32)
        staged[here, :] = (partial[here, :] + mixed).astype(BF16)
        copies.append(pltpu.make_async_copy(staged.at[here, :], out.at[here, :], sems.at[piece]))
        copies[-1].start()
    for copy in copies:
        copy.wait()


def cut_kernel(x, to_near, to_far, sems):
    even = lax.axis_index("seq") % 2 == 0
    count = to_near.shape[0]
    last = x.shape[0] - count
    near = pltpu.make_async_copy(x.at[pl.ds(pl.multiple_of(jnp.where(even, last, 0), 64), count), :], to_near, sems.at[0])
    far = pltpu.make_async_copy(x.at[pl.ds(pl.multiple_of(jnp.where(even, 0, last), 64), count), :], to_far, sems.at[1])
    near.start()
    far.start()
    near.wait()
    far.wait()


PIECES = 2


def call(kernel, outs, name, mebibytes, *operands, hbm=(), scratch=(), hbm_out=False):
    held, in_specs = [], []
    for i, operand in enumerate(operands):
        in_specs.append(ANY if i in hbm else VMEM)
        held.append(pltpu.with_memory_space_constraint(operand, pltpu.HBM if i in hbm else pltpu.VMEM))
    shapes = tuple((pltpu.HBM if hbm_out else pltpu.VMEM)(shape, dtype) for shape, dtype in outs)
    result = pl.pallas_call(
        kernel,
        out_shape=shapes,
        in_specs=in_specs,
        out_specs=(ANY if hbm_out else VMEM,) * len(shapes),
        scratch_shapes=list(scratch),
        compiler_params=pltpu.CompilerParams(vmem_limit_bytes=mebibytes << 20),
        name=name,
    )(*held)
    return result if len(outs) > 1 else result[0]


def local(seq_in, conv_gain, dw_kernel, mix_weight, attn_gain, q_weight, kv_weight, out_weight):
    rows, width = seq_in.shape
    taps = dw_kernel.shape[1]
    size = lax.axis_size("seq")
    first, second = rows // 8, rows // 4
    first_reach = taps // 2 * first
    reach1 = taps // 2 * second
    reach = first_reach + reach1
    mine = rows // 2
    lead = mine + 2 * reach1
    done = rows - 2 * first_reach

    near_pairs = [(i, i ^ 1) for i in range(size)]
    far_pairs = [(0, 0), (size - 1, size - 1)]
    for i in range(1, size - 1, 2):
        far_pairs += [(i, i + 1), (i + 1, i)]
    to_near, to_far = call(
        cut_kernel, [((reach, width), BF16)] * 2, "cut", 2, seq_in, hbm=(0,), scratch=[pltpu.SemaphoreType.DMA((2,))]
    )
    to_near, to_far, x_sent, mix_sent, out_sent = lax.optimization_barrier(
        (to_near, to_far, seq_in, mix_weight, out_weight)
    )
    near = lax.ppermute(to_near, "seq", near_pairs)
    far = lax.ppermute(to_far, "seq", far_pairs)

    small = jnp.concatenate(
        [conv_gain, dw_kernel.reshape(2 * taps, width), attn_gain[None, :], jnp.zeros((3, width), F32)], axis=0
    )
    small_peer = peer(small)
    x_peer = peer(x_sent)
    mix_peer = peer(mix_sent)
    out_peer = peer(out_sent)
    kv_flat = kv_weight.reshape(2 * width, 2 * kv_weight.shape[2])

    inner = call(
        functools.partial(inner_kernel, first=first, taps=taps),
        [
            ((2,) + small.shape, F32),
            ((2, rows, width), F32),
            ((2, done, width), F32),
            ((2, done, width), F32),
            ((2, 2, width, 2 * width), BF16),
        ],
        "inner",
        4,
        seq_in, x_peer, small, small_peer, mix_weight, mix_peer,
        hbm=(4, 5),
        scratch=[
            pltpu.VMEM((2, rows, width), BF16),
            pltpu.VMEM((2, done, width), BF16),
            pltpu.SemaphoreType.DMA((2, 2)),
        ],
    )
    near, far, kv_flat, *inner = lax.optimization_barrier((near, far, kv_flat, *inner))
    near_peer = peer(near)
    far_peer = peer(far)

    features, hidden_own, hidden_away = call(
        functools.partial(tower_kernel, first=first, second=second, length=rows * size, taps=taps),
        [((mine, 2 * width), BF16), ((mine, width), F32), ((mine, width), F32)],
        "tower",
        12,
        near, near_peer, far, far_peer, seq_in, x_peer, *inner,
        scratch=[
            pltpu.VMEM((2, rows + 2 * reach, width), BF16),
            pltpu.VMEM((2, rows + 2 * reach, width), F32),
            pltpu.VMEM((2, lead - done, width), F32),
            pltpu.VMEM((2, lead - done, width), BF16),
        ],
    )

    features_peer = peer(features)

    def project(weight, name):
        return call(
            project_kernel, [((rows, weight.shape[1]), BF16)], name, 4, features, features_peer, weight
        )

    kv = project(kv_flat, "keyvalue")
    order = ring_order(size)
    ahead = [(order[i], order[(i + 1) % size]) for i in range(size)]
    behind = [(b, a) for a, b in ahead]
    queries = None
    heads = q_weight.shape[1] // HD
    skip = [(order[i], order[(i + 2) % size]) for i in range(size)]
    skip_back = [(b, a) for a, b in skip]
    attend = functools.partial(attend_kernel, scale=1.0 / math.sqrt(HD))
    hidden_peer = peer(hidden_away)
    state, fresh = (), [kv]
    up = down = kv
    laps = size // 2 - 1
    for step in range(laps + 1):
        if step < laps:
            ahead_of, behind_of = up, down
            up = lax.ppermute(ahead_of, "seq", ahead)
            down = lax.ppermute(behind_of, "seq", behind)
            if step == laps - 1:
                halves = call(halve_kernel, [((rows // 2, kv.shape[1]), BF16)] * 2, "halve", 2, ahead_of, behind_of)
                opposite = [lax.ppermute(halves[0], "seq", skip), lax.ppermute(halves[1], "seq", skip_back)]
        if queries is None:
            queries = project(q_weight, "query")
        state = call(
            functools.partial(attend, count=len(fresh), first=step == 0, last=False),
            [((2 * heads, rows), F32), ((heads * HD, rows), F32)],
            "attend%d" % step,
            8,
            queries, *fresh, *state,
        )
        if step == 0:
            up, hidden_peer, *state = lax.optimization_barrier((up, hidden_peer, *state))
        elif step < laps:
            up, *state = lax.optimization_barrier((up, *state))
        if step < laps:
            down, *state = lax.optimization_barrier((down, *state))
            fresh = [up, down]
    context = call(
        functools.partial(attend, count=len(opposite), first=False, last=True),
        [((rows, heads * HD), BF16)],
        "attend_last",
        8,
        queries, *opposite, *state,
    )
    context_peer = peer(context)
    partial = call(
        begin_kernel, [((rows, width), F32)], "begin", 4, context, out_weight, hidden_own, hidden_peer
    )
    return call(
        finish_kernel, [((rows, width), BF16)], "finish", 4, context_peer, out_peer, partial,
        scratch=[pltpu.VMEM((rows, width), BF16), pltpu.SemaphoreType.DMA((PIECES,))], hbm_out=True,
    )


def solution(mesh):
    return jax.shard_map(
        local,
        mesh=mesh,
        in_specs=(
            P(("grp", "seq"), "ch"),
            P(None, "ch"),
            P(None, None, "ch"),
            P(None, "ch", None),
            P("ch"),
            P(None, "ch"),
            P(None, None, "ch"),
            P("ch", None),
        ),
        out_specs=P(("grp", "seq"), "ch"),
        check_vma=False,
    )
```

```python
import functools
import math

import jax
import jax.numpy as jnp
from jax import lax
from jax.experimental import pallas as pl
from jax.experimental.pallas import tpu as pltpu
from jax.sharding import PartitionSpec as P

HD = 128
EPSILON = 1e-06
BF16 = jnp.bfloat16
F32 = jnp.float32
SWAP = [(0, 1), (1, 0)]
VMEM = pl.BlockSpec(memory_space=pltpu.VMEM)
ANY = pl.BlockSpec(memory_space=pl.ANY)


def peer(array):
    return lax.ppermute(array, "ch", SWAP)


def ring_order(count):
    width = 1
    while width * width * 4 <= count:
        width *= 2
    rows = count // width
    if width == 1 or rows * width != count:
        return list(range(count))
    order = [row * width for row in range(rows)]
    for step, row in enumerate(reversed(range(rows))):
        columns = range(1, width) if step % 2 == 0 else range(width - 1, 0, -1)
        order += [row * width + column for column in columns]
    return order


def scale_of(parts, first_position, length):
    squares = jnp.sum(parts[0] * parts[0] + parts[1] * parts[1], axis=1, keepdims=True)
    scale = lax.rsqrt(squares / (2 * parts[0].shape[1]) + EPSILON)
    if first_position is None:
        return scale
    position = first_position + lax.broadcasted_iota(jnp.int32, scale.shape, 0)
    return jnp.where((position >= 0) & (position < length), scale, 0.0)


def convolve(normed, act, small, layer, source, to, dilation, taps):
    strip, width = 256, act.shape[2]
    for h in range(2):
        for column in range(0, width, strip):
            cols = slice(column, column + strip)
            total = None
            for tap in range(taps):
                row = 2 + layer * taps + tap
                at = source + tap * dilation
                term = normed[h, at : at + BLOCK, cols] * small[h, row : row + 1, cols]
                total = term if total is None else total + term
            act[h, to : to + BLOCK, cols] = jax.nn.gelu(total, approximate=True).astype(BF16)


def take_class(to, side, at, source, core, group):
    part = group // 2
    for i in range(source.shape[0] // group):
        first = pl.multiple_of(i * group + core * part, part)
        row = at + i * part
        if not isinstance(row, int):
            row = pl.multiple_of(row, part)
        to[side, pl.ds(row, part), :] = source[pl.ds(first, part), :]


def mix(act, weights, layer, count, half):
    width = act.shape[2]
    cols = pl.ds(half * width, width)
    mixed = jnp.dot(act[0, 0:count, :], weights[layer, 0, :, cols], preferred_element_type=F32)
    return mixed + jnp.dot(act[1, 0:count, :], weights[layer, 1, :, cols], preferred_element_type=F32)


BLOCK = 32


def inner_kernel(
    x_own, x_peer, small_own, small_peer, mix_own, mix_peer,
    small, normed, middle, middle_normed, weights, wide,
    act, sems, row_sems,
    *, first, taps,
):
    own = lax.axis_index("ch")
    other = 1 - own
    rows = wide.shape[1]
    dilation = first // 2
    reach = taps // 2 * dilation
    count = rows - 2 * reach
    mine = []
    part = first // 2
    for i in range(x_own.shape[0] // first):
        source = x_own.at[pl.ds(pl.multiple_of(i * first + own * part, part), part), :]
        mine.append(pltpu.make_async_copy(source, wide.at[own, pl.ds(i * part, part), :], row_sems.at[i]))
        mine[-1].start()
    copies = []
    for layer in range(2):
        for side, source, at in ((own, mix_own, 0), (other, mix_peer, 1)):
            copies.append(pltpu.make_async_copy(source.at[layer], weights.at[layer, side], sems.at[layer, at]))
            copies[-1].start()
    small[own] = small_own[...]
    small[other] = small_peer[...]
    take_class(wide, other, 0, x_peer, own, first)
    for copy in mine:
        copy.wait()
    for at in range(0, rows, BLOCK):
        here = slice(at, at + BLOCK)
        parts = [wide[h, here, :].astype(F32) for h in range(2)]
        scale = scale_of(parts, None, None)
        for h in range(2):
            normed[h, here, :] = parts[h] * scale * small[h, 0:1, :]
    for at in range(0, count, BLOCK):
        convolve(normed, act, small, 0, at, at, dilation, taps)
    copies[0].wait()
    copies[1].wait()
    for h in range(2):
        middle[h] = wide[h, reach : reach + count, :].astype(F32) + mix(act, weights, 0, count, h)
    for at in range(0, count, BLOCK):
        here = slice(at, at + BLOCK)
        parts = [middle[h, here, :] for h in range(2)]
        scale = scale_of(parts, None, None)
        for h in range(2):
            middle_normed[h, here, :] = parts[h] * scale * small[h, 1:2, :]
    copies[2].wait()
    copies[3].wait()


def tower_kernel(
    near_own, near_peer, far_own, far_peer, small, inner, inner_middle, inner_normed, weights, inner_wide,
    features, hidden_own, hidden_peer,
    wide, normed, middle, act,
    *, first, second, length, taps,
):
    own = lax.axis_index("ch")
    other = 1 - own
    even = lax.axis_index("seq") % 2 == 0
    width = near_own.shape[1]
    rows = inner_wide.shape[1]
    start = lax.axis_index("seq") * rows
    length = length // 2
    dilation, wider = first // 2, second // 2
    first_reach = taps // 2 * dilation
    reach1 = taps // 2 * wider
    reach = first_reach + reach1
    done = rows - 2 * first_reach
    lead = rows + 2 * reach1
    upper = reach1 + first_reach

    near_at = jnp.where(even, rows + reach, 0)
    far_at = jnp.where(even, 0, rows + reach)
    for side, near, far in ((own, near_own, far_own), (other, near_peer, far_peer)):
        take_class(wide, side, far_at, far, own, first)
        take_class(wide, side, near_at, near, own, first)
    for h in range(2):
        wide[h, reach : reach + rows, :] = inner_wide[h]
        normed[h, reach : reach + rows, :] = inner[h]

    halo_rows = [*range(0, reach, BLOCK), *range(reach + rows, 2 * reach + rows, BLOCK)]
    for at in halo_rows:
        here = slice(at, at + BLOCK)
        parts = [wide[h, here, :].astype(F32) for h in range(2)]
        scale = scale_of(parts, start - reach + at, length)
        for h in range(2):
            normed[h, here, :] = parts[h] * scale * small[h, 0:1, :]

    still = [*range(0, upper, BLOCK), *range(upper + done, lead, BLOCK)]
    for i, at in enumerate(still):
        convolve(normed, act, small, 0, at, i * BLOCK, dilation, taps)
    for h in range(2):
        middle[h] = mix(act, weights, 0, lead - done, h)

    for i, at in enumerate(still):
        here = slice(i * BLOCK, (i + 1) * BLOCK)
        parts = []
        for h in range(2):
            before = wide[h, first_reach + at : first_reach + at + BLOCK, :].astype(F32)
            parts.append(before + middle[h, here, :])
            middle[h, here, :] = parts[h]
        scale = scale_of(parts, start - reach1 + at, length)
        for h in range(2):
            normed[h, at : at + BLOCK, :] = parts[h] * scale * small[h, 1:2, :]
    for h in range(2):
        normed[h, upper : upper + done, :] = inner_normed[h]
    for at in range(0, rows, BLOCK):
        convolve(normed, act, small, 1, at, at, wider, taps)

    parts = []
    for h in range(2):
        before = jnp.concatenate(
            [middle[h, upper - first_reach : upper, :], inner_middle[h], middle[h, upper : upper + first_reach, :]], axis=0
        )
        parts.append(before + mix(act, weights, 1, rows, h))
        middle[h, 0:rows, :] = parts[h]
    hidden_own[...] = middle[own, 0:rows, :]
    hidden_peer[...] = middle[other, 0:rows, :]
    scale = scale_of(parts, None, None)
    last = 2 + 2 * taps
    for h in range(2):
        features[:, h * width : (h + 1) * width] = (parts[h] * scale * small[h, last : last + 1, :]).astype(BF16)


def project_kernel(own_ref, peer_ref, weight, out):
    count = own_ref.shape[0]
    own = lax.axis_index("ch")
    at = pl.multiple_of(own * count, count)
    back = pl.multiple_of((1 - own) * count, count)
    out[pl.ds(at, count), :] = jnp.dot(own_ref[...], weight[...], preferred_element_type=F32).astype(BF16)
    out[pl.ds(back, count), :] = jnp.dot(peer_ref[...], weight[...], preferred_element_type=F32).astype(BF16)


def halve_kernel(ahead, behind, upper, lower):
    count = upper.shape[0]
    upper[...] = ahead[0:count, :]
    lower[...] = behind[count:, :]


def attend_kernel(*refs, count, scale, first, last):
    q_ref, blocks, refs = refs[0], refs[1 : 1 + count], refs[1 + count :]
    state_in, refs = ((), refs) if first else (refs[:2], refs[2:])
    factor = scale * math.log2(math.e)
    heads = q_ref.shape[1] // HD
    for head in range(heads):
        cols = slice(head * HD, (head + 1) * HD)
        q = q_ref[:, cols]
        scores = [
            lax.dot_general(kv[:, 0:HD], q, (((1,), (1,)), ((), ())), preferred_element_type=F32) for kv in blocks
        ]
        peaks = [jnp.max(s, axis=0, keepdims=True) for s in scores]
        total = None
        context = None
        if not first:
            stats, summed = state_in
            before = stats[head : head + 1, :]
            peaks.append(before)
        peak = functools.reduce(jnp.maximum, peaks)
        if not first:
            keep = jnp.exp2((before - peak) * factor)
            total = stats[heads + head : heads + head + 1, :] * keep
            context = summed[cols, :] * keep
        for s, kv in zip(scores, blocks):
            probs = jnp.exp2((s - peak) * factor)
            part = jnp.sum(probs, axis=0, keepdims=True)
            value = lax.dot_general(
                kv[:, HD:], probs.astype(BF16), (((0,), (0,)), ((), ())), preferred_element_type=F32
            )
            total = part if total is None else total + part
            context = value if context is None else context + value
        if last:
            refs[0][:, cols] = jnp.transpose(context * (1.0 / total)).astype(BF16)
        else:
            refs[0][head : head + 1, :] = peak
            refs[0][heads + head : heads + head + 1, :] = total
            refs[1][cols, :] = context


def begin_kernel(ctx, w_own, hid_own, hid_peer, out):
    count, width = hid_own.shape
    own = lax.axis_index("ch")
    cols = pl.ds(pl.multiple_of(own * width, 128), width)
    for at, hid in ((own * count, hid_own), ((1 - own) * count, hid_peer)):
        rows = pl.ds(pl.multiple_of(at, count), count)
        out[rows, :] = hid[...] + jnp.dot(ctx[rows, :], w_own[:, cols], preferred_element_type=F32)


def finish_kernel(ctx, w_peer, partial, out, staged, sems):
    rows, width = partial.shape
    cols = pl.ds(pl.multiple_of(lax.axis_index("ch") * width, 128), width)
    groups, part = staged.shape[1:3]
    count = rows // 2
    copies = []
    for piece in range(2):
        here = slice(piece * count, (piece + 1) * count)
        mixed = jnp.dot(ctx[here, :], w_peer[:, cols], preferred_element_type=F32)
        value = (partial[here, :] + mixed).astype(BF16)
        for i in range(groups):
            staged[piece, i] = value[i * part : (i + 1) * part, :]
        copies.append(
            pltpu.make_async_copy(staged.at[piece], out.at[:, pl.ds(piece * part, part), :], sems.at[piece])
        )
        copies[-1].start()
    for copy in copies:
        copy.wait()


def cut_kernel(x, to_near, to_far, sems):
    even = lax.axis_index("seq") % 2 == 0
    count = to_near.shape[0]
    last = x.shape[0] - count
    near = pltpu.make_async_copy(x.at[pl.ds(pl.multiple_of(jnp.where(even, last, 0), 64), count), :], to_near, sems.at[0])
    far = pltpu.make_async_copy(x.at[pl.ds(pl.multiple_of(jnp.where(even, 0, last), 64), count), :], to_far, sems.at[1])
    near.start()
    far.start()
    near.wait()
    far.wait()


def call(kernel, outs, name, mebibytes, *operands, hbm=(), scratch=(), hbm_out=False):
    held, in_specs = [], []
    for i, operand in enumerate(operands):
        in_specs.append(ANY if i in hbm else VMEM)
        held.append(pltpu.with_memory_space_constraint(operand, pltpu.HBM if i in hbm else pltpu.VMEM))
    shapes = tuple((pltpu.HBM if hbm_out else pltpu.VMEM)(shape, dtype) for shape, dtype in outs)
    result = pl.pallas_call(
        kernel,
        out_shape=shapes,
        in_specs=in_specs,
        out_specs=(ANY if hbm_out else VMEM,) * len(shapes),
        scratch_shapes=list(scratch),
        compiler_params=pltpu.CompilerParams(vmem_limit_bytes=mebibytes << 20),
        name=name,
    )(*held)
    return result if len(outs) > 1 else result[0]


def local(seq_in, conv_gain, dw_kernel, mix_weight, attn_gain, q_weight, kv_weight, out_weight):
    rows, width = seq_in.shape
    taps = dw_kernel.shape[1]
    size = lax.axis_size("seq")
    first, second = rows // 8, rows // 4
    first_reach = taps // 2 * first
    reach1 = taps // 2 * second
    reach = first_reach + reach1
    mine = rows // 2
    done = mine - first_reach

    near_pairs = [(i, i ^ 1) for i in range(size)]
    far_pairs = [(0, 0), (size - 1, size - 1)]
    for i in range(1, size - 1, 2):
        far_pairs += [(i, i + 1), (i + 1, i)]
    to_near, to_far = call(
        cut_kernel, [((reach, width), BF16)] * 2, "cut", 2, seq_in, hbm=(0,), scratch=[pltpu.SemaphoreType.DMA((2,))]
    )
    to_near, to_far, x_sent, mix_sent, out_sent = lax.optimization_barrier(
        (to_near, to_far, seq_in, mix_weight, out_weight)
    )
    near = lax.ppermute(to_near, "seq", near_pairs)
    far = lax.ppermute(to_far, "seq", far_pairs)

    small = jnp.concatenate(
        [conv_gain, dw_kernel.reshape(2 * taps, width), attn_gain[None, :], jnp.zeros((3, width), F32)], axis=0
    )
    small_peer = peer(small)
    x_peer = peer(x_sent)
    mix_peer = peer(mix_sent)
    out_peer = peer(out_sent)
    kv_flat = kv_weight.reshape(2 * width, 2 * kv_weight.shape[2])

    inner = call(
        functools.partial(inner_kernel, first=first, taps=taps),
        [
            ((2,) + small.shape, F32),
            ((2, mine, width), F32),
            ((2, done, width), F32),
            ((2, done, width), F32),
            ((2, 2, width, 2 * width), BF16),
            ((2, mine, width), BF16),
        ],
        "inner",
        4,
        seq_in, x_peer, small, small_peer, mix_weight, mix_peer,
        hbm=(0, 4, 5),
        scratch=[
            pltpu.VMEM((2, done, width), BF16),
            pltpu.SemaphoreType.DMA((2, 2)),
            pltpu.SemaphoreType.DMA((rows // first,)),
        ],
    )
    near, far, kv_flat, *inner = lax.optimization_barrier((near, far, kv_flat, *inner))
    near_peer = peer(near)
    far_peer = peer(far)

    features, hidden_own, hidden_away = call(
        functools.partial(tower_kernel, first=first, second=second, length=rows * size, taps=taps),
        [((mine, 2 * width), BF16), ((mine, width), F32), ((mine, width), F32)],
        "tower",
        12,
        near, near_peer, far, far_peer, *inner,
        scratch=[
            pltpu.VMEM((2, mine + reach, width), BF16),
            pltpu.VMEM((2, mine + reach, width), F32),
            pltpu.VMEM((2, mine + reach1 - done, width), F32),
            pltpu.VMEM((2, mine + reach1 - done, width), BF16),
        ],
    )

    features_peer = peer(features)

    def project(weight, name):
        return call(
            project_kernel, [((rows, weight.shape[1]), BF16)], name, 4, features, features_peer, weight
        )

    kv = project(kv_flat, "keyvalue")
    order = ring_order(size)
    ahead = [(order[i], order[(i + 1) % size]) for i in range(size)]
    behind = [(b, a) for a, b in ahead]
    queries = None
    heads = q_weight.shape[1] // HD
    skip = [(order[i], order[(i + 2) % size]) for i in range(size)]
    skip_back = [(b, a) for a, b in skip]
    attend = functools.partial(attend_kernel, scale=1.0 / math.sqrt(HD))
    hidden_peer = peer(hidden_away)
    state, fresh = (), [kv]
    up = down = kv
    laps = size // 2 - 1
    for step in range(laps + 1):
        if step < laps:
            ahead_of, behind_of = up, down
            up = lax.ppermute(ahead_of, "seq", ahead)
            down = lax.ppermute(behind_of, "seq", behind)
            if step == laps - 1:
                halves = call(halve_kernel, [((rows // 2, kv.shape[1]), BF16)] * 2, "halve", 2, ahead_of, behind_of)
                opposite = [lax.ppermute(halves[0], "seq", skip), lax.ppermute(halves[1], "seq", skip_back)]
        if queries is None:
            queries = project(q_weight, "query")
        state = call(
            functools.partial(attend, count=len(fresh), first=step == 0, last=False),
            [((2 * heads, rows), F32), ((heads * HD, rows), F32)],
            "attend%d" % step,
            8,
            queries, *fresh, *state,
        )
        if step == 0:
            up, hidden_peer, *state = lax.optimization_barrier((up, hidden_peer, *state))
        elif step < laps:
            up, *state = lax.optimization_barrier((up, *state))
        if step < laps:
            down, *state = lax.optimization_barrier((down, *state))
            fresh = [up, down]
    context = call(
        functools.partial(attend, count=len(opposite), first=False, last=True),
        [((rows, heads * HD), BF16)],
        "attend_last",
        8,
        queries, *opposite, *state,
    )
    context_peer = peer(context)
    partial = call(
        begin_kernel, [((rows, width), F32)], "begin", 4, context, out_weight, hidden_own, hidden_peer
    )
    groups = rows // first
    out = call(
        finish_kernel, [((groups, first, width), BF16)], "finish", 4, context_peer, out_peer, partial,
        scratch=[pltpu.VMEM((2, groups, first // 2, width), BF16), pltpu.SemaphoreType.DMA((2,))], hbm_out=True,
    )
    return out.reshape(rows, width)


def solution(mesh):
    return jax.shard_map(
        local,
        mesh=mesh,
        in_specs=(
            P(("grp", "seq"), "ch"),
            P(None, "ch"),
            P(None, None, "ch"),
            P(None, "ch", None),
            P("ch"),
            P(None, "ch"),
            P(None, None, "ch"),
            P("ch", None),
        ),
        out_specs=P(("grp", "seq"), "ch"),
        check_vma=False,
    )
```

```python
import functools
import math

import jax
import jax.numpy as jnp
from jax import lax
from jax.experimental import pallas as pl
from jax.experimental.pallas import tpu as pltpu
from jax.sharding import PartitionSpec as P

HD = 128
EPSILON = 1e-06
BF16 = jnp.bfloat16
F32 = jnp.float32
SWAP = [(0, 1), (1, 0)]
VMEM = pl.BlockSpec(memory_space=pltpu.VMEM)
ANY = pl.BlockSpec(memory_space=pl.ANY)


def peer(array):
    return lax.ppermute(array, "ch", SWAP)


def ring_order(count):
    width = 1
    while width * width * 4 <= count:
        width *= 2
    rows = count // width
    if width == 1 or rows * width != count:
        return list(range(count))
    order = [row * width for row in range(rows)]
    for step, row in enumerate(reversed(range(rows))):
        columns = range(1, width) if step % 2 == 0 else range(width - 1, 0, -1)
        order += [row * width + column for column in columns]
    return order


def scale_of(parts, first_position, length):
    squares = jnp.sum(parts[0] * parts[0] + parts[1] * parts[1], axis=1, keepdims=True)
    scale = lax.rsqrt(squares / (2 * parts[0].shape[1]) + EPSILON)
    if first_position is None:
        return scale
    position = first_position + lax.broadcasted_iota(jnp.int32, scale.shape, 0)
    return jnp.where((position >= 0) & (position < length), scale, 0.0)


def convolve(normed, act, small, layer, source, to, dilation, taps):
    strip, width = 256, act.shape[2]
    for h in range(2):
        for column in range(0, width, strip):
            cols = slice(column, column + strip)
            total = None
            for tap in range(taps):
                row = 2 + layer * taps + tap
                at = source + tap * dilation
                term = normed[h, at : at + BLOCK, cols] * small[h, row : row + 1, cols]
                total = term if total is None else total + term
            act[h, to : to + BLOCK, cols] = jax.nn.gelu(total, approximate=True).astype(BF16)


def take_class(to, side, at, source, core, group):
    part = group // 2
    for i in range(source.shape[0] // group):
        first = pl.multiple_of(i * group + core * part, part)
        row = at + i * part
        if not isinstance(row, int):
            row = pl.multiple_of(row, part)
        to[side, pl.ds(row, part), :] = source[pl.ds(first, part), :]


def mix(act, weights, layer, count, half):
    width = act.shape[2]
    cols = pl.ds(half * width, width)
    mixed = jnp.dot(act[0, 0:count, :], weights[layer, 0, :, cols], preferred_element_type=F32)
    return mixed + jnp.dot(act[1, 0:count, :], weights[layer, 1, :, cols], preferred_element_type=F32)


BLOCK = 16


def inner_kernel(
    x_own, x_peer, small_own, small_peer, mix_own, mix_peer,
    small, normed, middle, middle_normed, weights, wide,
    act, sems, row_sems,
    *, first, taps,
):
    own = lax.axis_index("ch")
    other = 1 - own
    rows = wide.shape[1]
    dilation = first // 2
    reach = taps // 2 * dilation
    count = rows - 2 * reach
    mine = []
    part = first // 2
    for i in range(x_own.shape[0] // first):
        source = x_own.at[pl.ds(pl.multiple_of(i * first + own * part, part), part), :]
        mine.append(pltpu.make_async_copy(source, wide.at[own, pl.ds(i * part, part), :], row_sems.at[i]))
        mine[-1].start()
    copies = []
    for layer in range(2):
        for side, source, at in ((own, mix_own, 0), (other, mix_peer, 1)):
            copies.append(pltpu.make_async_copy(source.at[layer], weights.at[layer, side], sems.at[layer, at]))
            copies[-1].start()
    small[own] = small_own[...]
    small[other] = small_peer[...]
    take_class(wide, other, 0, x_peer, own, first)
    for copy in mine:
        copy.wait()
    for at in range(0, rows, BLOCK):
        here = slice(at, at + BLOCK)
        parts = [wide[h, here, :].astype(F32) for h in range(2)]
        scale = scale_of(parts, None, None)
        for h in range(2):
            normed[h, here, :] = parts[h] * scale * small[h, 0:1, :]
    for at in range(0, count, BLOCK):
        convolve(normed, act, small, 0, at, at, dilation, taps)
    copies[0].wait()
    copies[1].wait()
    for h in range(2):
        middle[h] = wide[h, reach : reach + count, :].astype(F32) + mix(act, weights, 0, count, h)
    for at in range(0, count, BLOCK):
        here = slice(at, at + BLOCK)
        parts = [middle[h, here, :] for h in range(2)]
        scale = scale_of(parts, None, None)
        for h in range(2):
            middle_normed[h, here, :] = parts[h] * scale * small[h, 1:2, :]
    copies[2].wait()
    copies[3].wait()


def tower_kernel(
    near_own, near_peer, far_own, far_peer, small, inner, inner_middle, inner_normed, weights, inner_wide,
    features, hidden_own, hidden_peer,
    wide, normed, middle, act,
    *, first, second, length, taps,
):
    own = lax.axis_index("ch")
    other = 1 - own
    even = lax.axis_index("seq") % 2 == 0
    width = near_own.shape[1]
    rows = inner_wide.shape[1]
    start = lax.axis_index("seq") * rows
    length = length // 2
    dilation, wider = first // 2, second // 2
    first_reach = taps // 2 * dilation
    reach1 = taps // 2 * wider
    reach = first_reach + reach1
    done = rows - 2 * first_reach
    lead = rows + 2 * reach1
    upper = reach1 + first_reach

    near_at = jnp.where(even, rows + reach, 0)
    far_at = jnp.where(even, 0, rows + reach)
    for side, near, far in ((own, near_own, far_own), (other, near_peer, far_peer)):
        take_class(wide, side, far_at, far, own, first)
        take_class(wide, side, near_at, near, own, first)
    for h in range(2):
        wide[h, reach : reach + rows, :] = inner_wide[h]
        normed[h, reach : reach + rows, :] = inner[h]

    halo_rows = [*range(0, reach, BLOCK), *range(reach + rows, 2 * reach + rows, BLOCK)]
    for at in halo_rows:
        here = slice(at, at + BLOCK)
        parts = [wide[h, here, :].astype(F32) for h in range(2)]
        scale = scale_of(parts, start - reach + at, length)
        for h in range(2):
            normed[h, here, :] = parts[h] * scale * small[h, 0:1, :]

    still = [*range(0, upper, BLOCK), *range(upper + done, lead, BLOCK)]
    for i, at in enumerate(still):
        convolve(normed, act, small, 0, at, i * BLOCK, dilation, taps)
    for h in range(2):
        middle[h] = mix(act, weights, 0, lead - done, h)

    for i, at in enumerate(still):
        here = slice(i * BLOCK, (i + 1) * BLOCK)
        parts = []
        for h in range(2):
            before = wide[h, first_reach + at : first_reach + at + BLOCK, :].astype(F32)
            parts.append(before + middle[h, here, :])
            middle[h, here, :] = parts[h]
        scale = scale_of(parts, start - reach1 + at, length)
        for h in range(2):
            normed[h, at : at + BLOCK, :] = parts[h] * scale * small[h, 1:2, :]
    for h in range(2):
        normed[h, upper : upper + done, :] = inner_normed[h]
    for at in range(0, rows, BLOCK):
        convolve(normed, act, small, 1, at, at, wider, taps)

    parts = []
    for h in range(2):
        before = jnp.concatenate(
            [middle[h, upper - first_reach : upper, :], inner_middle[h], middle[h, upper : upper + first_reach, :]], axis=0
        )
        parts.append(before + mix(act, weights, 1, rows, h))
        middle[h, 0:rows, :] = parts[h]
    hidden_own[...] = middle[own, 0:rows, :]
    hidden_peer[...] = middle[other, 0:rows, :]
    scale = scale_of(parts, None, None)
    last = 2 + 2 * taps
    for h in range(2):
        features[:, h * width : (h + 1) * width] = (parts[h] * scale * small[h, last : last + 1, :]).astype(BF16)


def project_kernel(own_ref, peer_ref, weight, out):
    count = own_ref.shape[0]
    own = lax.axis_index("ch")
    at = pl.multiple_of(own * count, count)
    back = pl.multiple_of((1 - own) * count, count)
    out[pl.ds(at, count), :] = jnp.dot(own_ref[...], weight[...], preferred_element_type=F32).astype(BF16)
    out[pl.ds(back, count), :] = jnp.dot(peer_ref[...], weight[...], preferred_element_type=F32).astype(BF16)


def halve_kernel(ahead, behind, upper, lower):
    count = upper.shape[0]
    upper[...] = ahead[0:count, :]
    lower[...] = behind[count:, :]


def attend_kernel(*refs, count, scale, first, last):
    q_ref, blocks, refs = refs[0], refs[1 : 1 + count], refs[1 + count :]
    state_in, refs = ((), refs) if first else (refs[:2], refs[2:])
    factor = scale * math.log2(math.e)
    heads = q_ref.shape[1] // HD
    for head in range(heads):
        cols = slice(head * HD, (head + 1) * HD)
        q = q_ref[:, cols]
        scores = [
            lax.dot_general(kv[:, 0:HD], q, (((1,), (1,)), ((), ())), preferred_element_type=F32) for kv in blocks
        ]
        peaks = [jnp.max(s, axis=0, keepdims=True) for s in scores]
        total = None
        context = None
        if not first:
            stats, summed = state_in
            before = stats[head : head + 1, :]
            peaks.append(before)
        peak = functools.reduce(jnp.maximum, peaks)
        if not first:
            keep = jnp.exp2((before - peak) * factor)
            total = stats[heads + head : heads + head + 1, :] * keep
            context = summed[cols, :] * keep
        for s, kv in zip(scores, blocks):
            probs = jnp.exp2((s - peak) * factor)
            part = jnp.sum(probs, axis=0, keepdims=True)
            value = lax.dot_general(
                kv[:, HD:], probs.astype(BF16), (((0,), (0,)), ((), ())), preferred_element_type=F32
            )
            total = part if total is None else total + part
            context = value if context is None else context + value
        if last:
            refs[0][:, cols] = jnp.transpose(context * (1.0 / total)).astype(BF16)
        else:
            refs[0][head : head + 1, :] = peak
            refs[0][heads + head : heads + head + 1, :] = total
            refs[1][cols, :] = context


def begin_kernel(ctx, w_own, hid_own, hid_peer, out):
    count, width = hid_own.shape
    own = lax.axis_index("ch")
    cols = pl.ds(pl.multiple_of(own * width, 128), width)
    for at, hid in ((own * count, hid_own), ((1 - own) * count, hid_peer)):
        rows = pl.ds(pl.multiple_of(at, count), count)
        out[rows, :] = hid[...] + jnp.dot(ctx[rows, :], w_own[:, cols], preferred_element_type=F32)


def finish_kernel(ctx, w_peer, partial, out, staged, sems):
    rows, width = partial.shape
    cols = pl.ds(pl.multiple_of(lax.axis_index("ch") * width, 128), width)
    groups, part = staged.shape[1:3]
    count = rows // 2
    copies = []
    for piece in range(2):
        here = slice(piece * count, (piece + 1) * count)
        mixed = jnp.dot(ctx[here, :], w_peer[:, cols], preferred_element_type=F32)
        value = (partial[here, :] + mixed).astype(BF16)
        for i in range(groups):
            staged[piece, i] = value[i * part : (i + 1) * part, :]
        copies.append(
            pltpu.make_async_copy(staged.at[piece], out.at[:, pl.ds(piece * part, part), :], sems.at[piece])
        )
        copies[-1].start()
    for copy in copies:
        copy.wait()


def cut_kernel(x, to_near, to_far, sems):
    even = lax.axis_index("seq") % 2 == 0
    count = to_near.shape[0]
    last = x.shape[0] - count
    near = pltpu.make_async_copy(x.at[pl.ds(pl.multiple_of(jnp.where(even, last, 0), 64), count), :], to_near, sems.at[0])
    far = pltpu.make_async_copy(x.at[pl.ds(pl.multiple_of(jnp.where(even, 0, last), 64), count), :], to_far, sems.at[1])
    near.start()
    far.start()
    near.wait()
    far.wait()


def call(kernel, outs, name, mebibytes, *operands, hbm=(), scratch=(), hbm_out=False):
    held, in_specs = [], []
    for i, operand in enumerate(operands):
        in_specs.append(ANY if i in hbm else VMEM)
        held.append(pltpu.with_memory_space_constraint(operand, pltpu.HBM if i in hbm else pltpu.VMEM))
    shapes = tuple((pltpu.HBM if hbm_out else pltpu.VMEM)(shape, dtype) for shape, dtype in outs)
    result = pl.pallas_call(
        kernel,
        out_shape=shapes,
        in_specs=in_specs,
        out_specs=(ANY if hbm_out else VMEM,) * len(shapes),
        scratch_shapes=list(scratch),
        compiler_params=pltpu.CompilerParams(vmem_limit_bytes=mebibytes << 20),
        name=name,
    )(*held)
    return result if len(outs) > 1 else result[0]


def local(seq_in, conv_gain, dw_kernel, mix_weight, attn_gain, q_weight, kv_weight, out_weight):
    rows, width = seq_in.shape
    taps = dw_kernel.shape[1]
    size = lax.axis_size("seq")
    first, second = rows // 8, rows // 4
    first_reach = taps // 2 * first
    reach1 = taps // 2 * second
    reach = first_reach + reach1
    mine = rows // 2
    done = mine - first_reach

    near_pairs = [(i, i ^ 1) for i in range(size)]
    far_pairs = [(0, size - 1), (size - 1, 0)]
    for i in range(1, size - 1, 2):
        far_pairs += [(i, i + 1), (i + 1, i)]
    to_near, to_far = call(
        cut_kernel, [((reach, width), BF16)] * 2, "cut", 2, seq_in, hbm=(0,), scratch=[pltpu.SemaphoreType.DMA((2,))]
    )
    to_near, to_far, x_sent, mix_sent, out_sent = lax.optimization_barrier(
        (to_near, to_far, seq_in, mix_weight, out_weight)
    )
    near = lax.ppermute(to_near, "seq", near_pairs)
    far = lax.ppermute(to_far, "seq", far_pairs)

    small = jnp.concatenate(
        [conv_gain, dw_kernel.reshape(2 * taps, width), attn_gain[None, :], jnp.zeros((3, width), F32)], axis=0
    )
    small_peer = peer(small)
    x_peer = peer(x_sent)
    mix_peer = peer(mix_sent)
    out_peer = peer(out_sent)
    kv_flat = kv_weight.reshape(2 * width, 2 * kv_weight.shape[2])

    inner = call(
        functools.partial(inner_kernel, first=first, taps=taps),
        [
            ((2,) + small.shape, F32),
            ((2, mine, width), F32),
            ((2, done, width), F32),
            ((2, done, width), F32),
            ((2, 2, width, 2 * width), BF16),
            ((2, mine, width), BF16),
        ],
        "inner",
        4,
        seq_in, x_peer, small, small_peer, mix_weight, mix_peer,
        hbm=(0, 4, 5),
        scratch=[
            pltpu.VMEM((2, done, width), BF16),
            pltpu.SemaphoreType.DMA((2, 2)),
            pltpu.SemaphoreType.DMA((rows // first,)),
        ],
    )
    near, far, kv_flat, *inner = lax.optimization_barrier((near, far, kv_flat, *inner))
    near_peer = peer(near)
    far_peer = peer(far)

    features, hidden_own, hidden_away = call(
        functools.partial(tower_kernel, first=first, second=second, length=rows * size, taps=taps),
        [((mine, 2 * width), BF16), ((mine, width), F32), ((mine, width), F32)],
        "tower",
        12,
        near, near_peer, far, far_peer, *inner,
        scratch=[
            pltpu.VMEM((2, mine + reach, width), BF16),
            pltpu.VMEM((2, mine + reach, width), F32),
            pltpu.VMEM((2, mine + reach1 - done, width), F32),
            pltpu.VMEM((2, mine + reach1 - done, width), BF16),
        ],
    )

    features_peer = peer(features)

    def project(weight, name):
        return call(
            project_kernel, [((rows, weight.shape[1]), BF16)], name, 4, features, features_peer, weight
        )

    kv = project(kv_flat, "keyvalue")
    order = ring_order(size)
    ahead = [(order[i], order[(i + 1) % size]) for i in range(size)]
    behind = [(b, a) for a, b in ahead]
    queries = None
    heads = q_weight.shape[1] // HD
    skip = [(order[i], order[(i + 2) % size]) for i in range(size)]
    skip_back = [(b, a) for a, b in skip]
    attend = functools.partial(attend_kernel, scale=1.0 / math.sqrt(HD))
    hidden_peer = peer(hidden_away)
    state, fresh = (), [kv]
    up = down = kv
    laps = size // 2 - 1
    for step in range(laps + 1):
        if step < laps:
            ahead_of, behind_of = up, down
            up = lax.ppermute(ahead_of, "seq", ahead)
            down = lax.ppermute(behind_of, "seq", behind)
            if step == laps - 1:
                halves = call(halve_kernel, [((rows // 2, kv.shape[1]), BF16)] * 2, "halve", 2, ahead_of, behind_of)
                opposite = [lax.ppermute(halves[0], "seq", skip), lax.ppermute(halves[1], "seq", skip_back)]
        if queries is None:
            queries = project(q_weight, "query")
        state = call(
            functools.partial(attend, count=len(fresh), first=step == 0, last=False),
            [((2 * heads, rows), F32), ((heads * HD, rows), F32)],
            "attend%d" % step,
            8,
            queries, *fresh, *state,
        )
        if step == 0:
            up, hidden_peer, *state = lax.optimization_barrier((up, hidden_peer, *state))
        elif step < laps:
            up, *state = lax.optimization_barrier((up, *state))
        if step < laps:
            down, *state = lax.optimization_barrier((down, *state))
            fresh = [up, down]
    context = call(
        functools.partial(attend, count=len(opposite), first=False, last=True),
        [((rows, heads * HD), BF16)],
        "attend_last",
        8,
        queries, *opposite, *state,
    )
    context_peer = peer(context)
    partial = call(
        begin_kernel, [((rows, width), F32)], "begin", 4, context, out_weight, hidden_own, hidden_peer
    )
    groups = rows // first
    out = call(
        finish_kernel, [((groups, first, width), BF16)], "finish", 4, context_peer, out_peer, partial,
        scratch=[pltpu.VMEM((2, groups, first // 2, width), BF16), pltpu.SemaphoreType.DMA((2,))], hbm_out=True,
    )
    return out.reshape(rows, width)


def solution(mesh):
    return jax.shard_map(
        local,
        mesh=mesh,
        in_specs=(
            P(("grp", "seq"), "ch"),
            P(None, "ch"),
            P(None, None, "ch"),
            P(None, "ch", None),
            P("ch"),
            P(None, "ch"),
            P(None, None, "ch"),
            P("ch", None),
        ),
        out_specs=P(("grp", "seq"), "ch"),
        check_vma=False,
    )
```

```python
import functools
import math

import jax
import jax.numpy as jnp
from jax import lax
from jax.experimental import pallas as pl
from jax.experimental.pallas import tpu as pltpu
from jax.sharding import PartitionSpec as P

HD = 128
EPSILON = 1e-06
BF16 = jnp.bfloat16
F32 = jnp.float32
SWAP = [(0, 1), (1, 0)]
VMEM = pl.BlockSpec(memory_space=pltpu.VMEM)
ANY = pl.BlockSpec(memory_space=pl.ANY)


def peer(array):
    return lax.ppermute(array, "ch", SWAP)


def ring_order(count):
    width = 1
    while width * width * 4 <= count:
        width *= 2
    rows = count // width
    if width == 1 or rows * width != count:
        return list(range(count))
    order = [row * width for row in range(rows)]
    for step, row in enumerate(reversed(range(rows))):
        columns = range(1, width) if step % 2 == 0 else range(width - 1, 0, -1)
        order += [row * width + column for column in columns]
    return order


def scale_of(parts, first_position, length):
    squares = jnp.sum(parts[0] * parts[0] + parts[1] * parts[1], axis=1, keepdims=True)
    scale = lax.rsqrt(squares / (2 * parts[0].shape[1]) + EPSILON)
    if first_position is None:
        return scale
    position = first_position + lax.broadcasted_iota(jnp.int32, scale.shape, 0)
    return jnp.where((position >= 0) & (position < length), scale, 0.0)


def convolve(normed, act, small, layer, source, to, dilation, taps):
    strip, width = 256, act.shape[2]
    for h in range(2):
        for column in range(0, width, strip):
            cols = slice(column, column + strip)
            total = None
            for tap in range(taps):
                row = 2 + layer * taps + tap
                at = source + tap * dilation
                term = normed[h, at : at + BLOCK, cols] * small[h, row : row + 1, cols]
                total = term if total is None else total + term
            act[h, to : to + BLOCK, cols] = jax.nn.gelu(total, approximate=True).astype(BF16)


def take_class(to, side, source, core, group):
    part = group // 2
    for i in range(source.shape[0] // group):
        first = pl.multiple_of(i * group + core * part, part)
        to[side, i * part : (i + 1) * part, :] = source[pl.ds(first, part), :]


def mix(act, weights, layer, count, half):
    width = act.shape[2]
    cols = pl.ds(half * width, width)
    mixed = jnp.dot(act[0, 0:count, :], weights[layer, 0, :, cols], preferred_element_type=F32)
    return mixed + jnp.dot(act[1, 0:count, :], weights[layer, 1, :, cols], preferred_element_type=F32)


BLOCK = 32


def inner_kernel(
    x_own, x_peer, small_own, small_peer, mix_own, mix_peer,
    small, normed, middle, middle_normed, weights, wide,
    act, sems, row_sems,
    *, first, taps,
):
    own = lax.axis_index("ch")
    other = 1 - own
    rows = wide.shape[1]
    dilation = first // 2
    reach = taps // 2 * dilation
    count = rows - 2 * reach
    mine = []
    part = first // 2
    for i in range(x_own.shape[0] // first):
        source = x_own.at[pl.ds(pl.multiple_of(i * first + own * part, part), part), :]
        mine.append(pltpu.make_async_copy(source, wide.at[own, pl.ds(i * part, part), :], row_sems.at[i]))
        mine[-1].start()
    copies = []
    for layer in range(2):
        for side, source, at in ((own, mix_own, 0), (other, mix_peer, 1)):
            copies.append(pltpu.make_async_copy(source.at[layer], weights.at[layer, side], sems.at[layer, at]))
            copies[-1].start()
    small[own] = small_own[...]
    small[other] = small_peer[...]
    take_class(wide, other, x_peer, own, first)
    for copy in mine:
        copy.wait()
    for at in range(0, rows, BLOCK):
        here = slice(at, at + BLOCK)
        parts = [wide[h, here, :].astype(F32) for h in range(2)]
        scale = scale_of(parts, None, None)
        for h in range(2):
            normed[h, here, :] = parts[h] * scale * small[h, 0:1, :]
    for at in range(0, count, BLOCK):
        convolve(normed, act, small, 0, at, at, dilation, taps)
    copies[0].wait()
    copies[1].wait()
    for h in range(2):
        middle[h] = wide[h, reach : reach + count, :].astype(F32) + mix(act, weights, 0, count, h)
    for at in range(0, count, BLOCK):
        here = slice(at, at + BLOCK)
        parts = [middle[h, here, :] for h in range(2)]
        scale = scale_of(parts, None, None)
        for h in range(2):
            middle_normed[h, here, :] = parts[h] * scale * small[h, 1:2, :]
    copies[2].wait()
    copies[3].wait()


def tower_kernel(
    near, far, small, inner, inner_middle, inner_normed, weights, inner_wide,
    features, hidden_own, hidden_peer,
    wide, normed, middle, act,
    *, first, second, length, taps,
):
    own = lax.axis_index("ch")
    other = 1 - own
    even = lax.axis_index("seq") % 2 == 0
    width = near.shape[2]
    rows = inner_wide.shape[1]
    start = lax.axis_index("seq") * rows
    length = length // 2
    dilation, wider = first // 2, second // 2
    first_reach = taps // 2 * dilation
    reach1 = taps // 2 * wider
    reach = first_reach + reach1
    done = rows - 2 * first_reach
    lead = rows + 2 * reach1
    upper = reach1 + first_reach

    near_at = jnp.where(even, rows + reach, 0)
    far_at = jnp.where(even, 0, rows + reach)
    for half, side in enumerate((own, other)):
        wide[side, pl.ds(pl.multiple_of(far_at, BLOCK), reach), :] = far[half]
        wide[side, pl.ds(pl.multiple_of(near_at, BLOCK), reach), :] = near[half]
    for h in range(2):
        wide[h, reach : reach + rows, :] = inner_wide[h]
        normed[h, reach : reach + rows, :] = inner[h]

    halo_rows = [*range(0, reach, BLOCK), *range(reach + rows, 2 * reach + rows, BLOCK)]
    for at in halo_rows:
        here = slice(at, at + BLOCK)
        parts = [wide[h, here, :].astype(F32) for h in range(2)]
        scale = scale_of(parts, start - reach + at, length)
        for h in range(2):
            normed[h, here, :] = parts[h] * scale * small[h, 0:1, :]

    still = [*range(0, upper, BLOCK), *range(upper + done, lead, BLOCK)]
    for i, at in enumerate(still):
        convolve(normed, act, small, 0, at, i * BLOCK, dilation, taps)
    for h in range(2):
        middle[h] = mix(act, weights, 0, lead - done, h)

    for i, at in enumerate(still):
        here = slice(i * BLOCK, (i + 1) * BLOCK)
        parts = []
        for h in range(2):
            before = wide[h, first_reach + at : first_reach + at + BLOCK, :].astype(F32)
            parts.append(before + middle[h, here, :])
            middle[h, here, :] = parts[h]
        scale = scale_of(parts, start - reach1 + at, length)
        for h in range(2):
            normed[h, at : at + BLOCK, :] = parts[h] * scale * small[h, 1:2, :]
    for h in range(2):
        normed[h, upper : upper + done, :] = inner_normed[h]
    for at in range(0, rows, BLOCK):
        convolve(normed, act, small, 1, at, at, wider, taps)

    parts = []
    for h in range(2):
        before = jnp.concatenate(
            [middle[h, upper - first_reach : upper, :], inner_middle[h], middle[h, upper : upper + first_reach, :]], axis=0
        )
        parts.append(before + mix(act, weights, 1, rows, h))
        middle[h, 0:rows, :] = parts[h]
    hidden_own[...] = middle[own, 0:rows, :]
    hidden_peer[...] = middle[other, 0:rows, :]
    scale = scale_of(parts, None, None)
    last = 2 + 2 * taps
    for h in range(2):
        features[:, h * width : (h + 1) * width] = (parts[h] * scale * small[h, last : last + 1, :]).astype(BF16)


def project_kernel(own_ref, peer_ref, weight, out):
    count = own_ref.shape[0]
    own = lax.axis_index("ch")
    at = pl.multiple_of(own * count, count)
    back = pl.multiple_of((1 - own) * count, count)
    out[pl.ds(at, count), :] = jnp.dot(own_ref[...], weight[...], preferred_element_type=F32).astype(BF16)
    out[pl.ds(back, count), :] = jnp.dot(peer_ref[...], weight[...], preferred_element_type=F32).astype(BF16)


def halve_kernel(ahead, behind, upper, lower):
    count = upper.shape[0]
    upper[...] = ahead[0:count, :]
    lower[...] = behind[count:, :]


def attend_kernel(*refs, count, scale, first, last):
    q_ref, blocks, refs = refs[0], refs[1 : 1 + count], refs[1 + count :]
    state_in, refs = ((), refs) if first else (refs[:2], refs[2:])
    factor = scale * math.log2(math.e)
    heads = q_ref.shape[1] // HD
    for head in range(heads):
        cols = slice(head * HD, (head + 1) * HD)
        q = q_ref[:, cols]
        scores = [
            lax.dot_general(kv[:, 0:HD], q, (((1,), (1,)), ((), ())), preferred_element_type=F32) for kv in blocks
        ]
        peaks = [jnp.max(s, axis=0, keepdims=True) for s in scores]
        total = None
        context = None
        if not first:
            stats, summed = state_in
            before = stats[head : head + 1, :]
            peaks.append(before)
        peak = functools.reduce(jnp.maximum, peaks)
        if not first:
            keep = jnp.exp2((before - peak) * factor)
            total = stats[heads + head : heads + head + 1, :] * keep
            context = summed[cols, :] * keep
        for s, kv in zip(scores, blocks):
            probs = jnp.exp2((s - peak) * factor)
            part = jnp.sum(probs, axis=0, keepdims=True)
            value = lax.dot_general(
                kv[:, HD:], probs.astype(BF16), (((0,), (0,)), ((), ())), preferred_element_type=F32
            )
            total = part if total is None else total + part
            context = value if context is None else context + value
        if last:
            refs[0][:, cols] = jnp.transpose(context * (1.0 / total)).astype(BF16)
        else:
            refs[0][head : head + 1, :] = peak
            refs[0][heads + head : heads + head + 1, :] = total
            refs[1][cols, :] = context


def begin_kernel(ctx, w_own, hid_own, hid_peer, out):
    count, width = hid_own.shape
    own = lax.axis_index("ch")
    cols = pl.ds(pl.multiple_of(own * width, 128), width)
    for at, hid in ((own * count, hid_own), ((1 - own) * count, hid_peer)):
        rows = pl.ds(pl.multiple_of(at, count), count)
        out[rows, :] = hid[...] + jnp.dot(ctx[rows, :], w_own[:, cols], preferred_element_type=F32)


def finish_kernel(ctx, w_peer, partial, out, staged, sems):
    rows, width = partial.shape
    cols = pl.ds(pl.multiple_of(lax.axis_index("ch") * width, 128), width)
    groups, part = staged.shape[1:3]
    count = rows // 2
    copies = []
    for piece in range(2):
        here = slice(piece * count, (piece + 1) * count)
        mixed = jnp.dot(ctx[here, :], w_peer[:, cols], preferred_element_type=F32)
        value = (partial[here, :] + mixed).astype(BF16)
        for i in range(groups):
            staged[piece, i] = value[i * part : (i + 1) * part, :]
        copies.append(
            pltpu.make_async_copy(staged.at[piece], out.at[:, pl.ds(piece * part, part), :], sems.at[piece])
        )
        copies[-1].start()
    for copy in copies:
        copy.wait()


def bring_kernel(x, to, sem):
    copy = pltpu.make_async_copy(x, to, sem)
    copy.start()
    copy.wait()


def cut_kernel(x_own, x_peer, near, far, sems):
    even = lax.axis_index("seq") % 2 == 0
    count, part = near.shape[1:3]
    last = x_own.shape[0] - count
    rows = pl.ds(pl.multiple_of(lax.axis_index("ch") * part, part), part)
    copies = []
    for half, x in enumerate((x_own, x_peer)):
        for to, begin in ((near, jnp.where(even, last, 0)), (far, jnp.where(even, 0, last))):
            source = x.at[pl.ds(begin, count), rows, :]
            copies.append(pltpu.make_async_copy(source, to.at[half], sems.at[len(copies)]))
            copies[-1].start()
    for copy in copies:
        copy.wait()


def call(kernel, outs, name, mebibytes, *operands, hbm=(), scratch=(), hbm_out=False):
    held, in_specs = [], []
    for i, operand in enumerate(operands):
        in_specs.append(ANY if i in hbm else VMEM)
        held.append(pltpu.with_memory_space_constraint(operand, pltpu.HBM if i in hbm else pltpu.VMEM))
    shapes = tuple((pltpu.HBM if hbm_out else pltpu.VMEM)(shape, dtype) for shape, dtype in outs)
    result = pl.pallas_call(
        kernel,
        out_shape=shapes,
        in_specs=in_specs,
        out_specs=(ANY if hbm_out else VMEM,) * len(shapes),
        scratch_shapes=list(scratch),
        compiler_params=pltpu.CompilerParams(vmem_limit_bytes=mebibytes << 20),
        name=name,
    )(*held)
    return result if len(outs) > 1 else result[0]


def local(seq_in, conv_gain, dw_kernel, mix_weight, attn_gain, q_weight, kv_weight, out_weight):
    rows, width = seq_in.shape
    taps = dw_kernel.shape[1]
    size = lax.axis_size("seq")
    first, second = rows // 8, rows // 4
    first_reach = taps // 2 * first
    reach1 = taps // 2 * second
    reach = first_reach + reach1
    mine = rows // 2
    done = mine - first_reach

    near_pairs = [(i, i ^ 1) for i in range(size)]
    far_pairs = [(0, 0), (size - 1, size - 1)]
    for i in range(1, size - 1, 2):
        far_pairs += [(i, i + 1), (i + 1, i)]
    x_here = call(bring_kernel, [((rows, width), BF16)], "bring", 2, seq_in, hbm=(0,), scratch=[pltpu.SemaphoreType.DMA(())])
    x_peer, x_here, mix_sent, out_sent = lax.optimization_barrier((peer(seq_in), x_here, mix_weight, out_weight))
    groups = rows // first
    cuts = call(
        cut_kernel,
        [((2, reach // first, first // 2, width), BF16)] * 2,
        "cut",
        2,
        x_here.reshape(groups, first, width),
        x_peer.reshape(groups, first, width),
        scratch=[pltpu.SemaphoreType.DMA((4,))],
    )
    to_near, to_far = (part.reshape(2, reach // 2, width) for part in cuts)
    to_near, to_far, mix_sent, out_sent = lax.optimization_barrier((to_near, to_far, mix_sent, out_sent))
    near = lax.ppermute(to_near, "seq", near_pairs)
    far = lax.ppermute(to_far, "seq", far_pairs)

    small = jnp.concatenate(
        [conv_gain, dw_kernel.reshape(2 * taps, width), attn_gain[None, :], jnp.zeros((3, width), F32)], axis=0
    )
    small_peer = peer(small)
    mix_peer = peer(mix_sent)
    out_peer = peer(out_sent)
    kv_flat = kv_weight.reshape(2 * width, 2 * kv_weight.shape[2])

    inner = call(
        functools.partial(inner_kernel, first=first, taps=taps),
        [
            ((2,) + small.shape, F32),
            ((2, mine, width), F32),
            ((2, done, width), F32),
            ((2, done, width), F32),
            ((2, 2, width, 2 * width), BF16),
            ((2, mine, width), BF16),
        ],
        "inner",
        4,
        seq_in, x_peer, small, small_peer, mix_weight, mix_peer,
        hbm=(0, 4, 5),
        scratch=[
            pltpu.VMEM((2, done, width), BF16),
            pltpu.SemaphoreType.DMA((2, 2)),
            pltpu.SemaphoreType.DMA((rows // first,)),
        ],
    )
    near, far, kv_flat, *inner = lax.optimization_barrier((near, far, kv_flat, *inner))

    features, hidden_own, hidden_away = call(
        functools.partial(tower_kernel, first=first, second=second, length=rows * size, taps=taps),
        [((mine, 2 * width), BF16), ((mine, width), F32), ((mine, width), F32)],
        "tower",
        12,
        near, far, *inner,
        scratch=[
            pltpu.VMEM((2, mine + reach, width), BF16),
            pltpu.VMEM((2, mine + reach, width), F32),
            pltpu.VMEM((2, mine + reach1 - done, width), F32),
            pltpu.VMEM((2, mine + reach1 - done, width), BF16),
        ],
    )

    features_peer = peer(features)

    def project(weight, name):
        return call(
            project_kernel, [((rows, weight.shape[1]), BF16)], name, 4, features, features_peer, weight
        )

    kv = project(kv_flat, "keyvalue")
    order = ring_order(size)
    ahead = [(order[i], order[(i + 1) % size]) for i in range(size)]
    behind = [(b, a) for a, b in ahead]
    queries = None
    heads = q_weight.shape[1] // HD
    skip = [(order[i], order[(i + 2) % size]) for i in range(size)]
    skip_back = [(b, a) for a, b in skip]
    attend = functools.partial(attend_kernel, scale=1.0 / math.sqrt(HD))
    hidden_peer = peer(hidden_away)
    state, fresh = (), [kv]
    up = down = kv
    laps = size // 2 - 1
    for step in range(laps + 1):
        if step < laps:
            ahead_of, behind_of = up, down
            up = lax.ppermute(ahead_of, "seq", ahead)
            down = lax.ppermute(behind_of, "seq", behind)
            if step == laps - 1:
                halves = call(halve_kernel, [((rows // 2, kv.shape[1]), BF16)] * 2, "halve", 2, ahead_of, behind_of)
                opposite = [lax.ppermute(halves[0], "seq", skip), lax.ppermute(halves[1], "seq", skip_back)]
        if queries is None:
            queries = project(q_weight, "query")
        state = call(
            functools.partial(attend, count=len(fresh), first=step == 0, last=False),
            [((2 * heads, rows), F32), ((heads * HD, rows), F32)],
            "attend%d" % step,
            8,
            queries, *fresh, *state,
        )
        if step == 0:
            up, hidden_peer, *state = lax.optimization_barrier((up, hidden_peer, *state))
        elif step < laps:
            up, *state = lax.optimization_barrier((up, *state))
        if step < laps:
            down, *state = lax.optimization_barrier((down, *state))
            fresh = [up, down]
    context = call(
        functools.partial(attend, count=len(opposite), first=False, last=True),
        [((rows, heads * HD), BF16)],
        "attend_last",
        8,
        queries, *opposite, *state,
    )
    context_peer = peer(context)
    partial = call(
        begin_kernel, [((rows, width), F32)], "begin", 4, context, out_weight, hidden_own, hidden_peer
    )
    groups = rows // first
    out = call(
        finish_kernel, [((groups, first, width), BF16)], "finish", 4, context_peer, out_peer, partial,
        scratch=[pltpu.VMEM((2, groups, first // 2, width), BF16), pltpu.SemaphoreType.DMA((2,))], hbm_out=True,
    )
    return out.reshape(rows, width)


def solution(mesh):
    return jax.shard_map(
        local,
        mesh=mesh,
        in_specs=(
            P(("grp", "seq"), "ch"),
            P(None, "ch"),
            P(None, None, "ch"),
            P(None, "ch", None),
            P("ch"),
            P(None, "ch"),
            P(None, None, "ch"),
            P("ch", None),
        ),
        out_specs=P(("grp", "seq"), "ch"),
        check_vma=False,
    )
```

```python
import functools
import math

import jax
import jax.numpy as jnp
from jax import lax
from jax.experimental import pallas as pl
from jax.experimental.pallas import tpu as pltpu
from jax.sharding import PartitionSpec as P

HD = 128
EPSILON = 1e-06
BF16 = jnp.bfloat16
F32 = jnp.float32
SWAP = [(0, 1), (1, 0)]
VMEM = pl.BlockSpec(memory_space=pltpu.VMEM)
ANY = pl.BlockSpec(memory_space=pl.ANY)


def peer(array):
    return lax.ppermute(array, "ch", SWAP)


def ring_order(count):
    width = 1
    while width * width * 4 <= count:
        width *= 2
    rows = count // width
    if width == 1 or rows * width != count:
        return list(range(count))
    order = [row * width for row in range(rows)]
    for step, row in enumerate(reversed(range(rows))):
        columns = range(1, width) if step % 2 == 0 else range(width - 1, 0, -1)
        order += [row * width + column for column in columns]
    return order


def scale_of(parts, first_position, length):
    squares = jnp.sum(parts[0] * parts[0] + parts[1] * parts[1], axis=1, keepdims=True)
    scale = lax.rsqrt(squares / (2 * parts[0].shape[1]) + EPSILON)
    if first_position is None:
        return scale
    position = first_position + lax.broadcasted_iota(jnp.int32, scale.shape, 0)
    return jnp.where((position >= 0) & (position < length), scale, 0.0)


def convolve(normed, act, small, layer, source, to, dilation, taps):
    strip, width = 256, act.shape[2]
    for h in range(2):
        for column in range(0, width, strip):
            cols = slice(column, column + strip)
            total = None
            for tap in range(taps):
                row = 2 + layer * taps + tap
                at = source + tap * dilation
                term = normed[h, at : at + BLOCK, cols] * small[h, row : row + 1, cols]
                total = term if total is None else total + term
            act[h, to : to + BLOCK, cols] = jax.nn.gelu(total, approximate=True).astype(BF16)


def take_class(to, side, source, core, group):
    part = group // 2
    for i in range(source.shape[0] // group):
        first = pl.multiple_of(i * group + core * part, part)
        to[side, i * part : (i + 1) * part, :] = source[pl.ds(first, part), :]


def mix(act, weights, layer, count, half):
    width = act.shape[2]
    cols = pl.ds(half * width, width)
    mixed = jnp.dot(act[0, 0:count, :], weights[layer, 0, :, cols], preferred_element_type=F32)
    return mixed + jnp.dot(act[1, 0:count, :], weights[layer, 1, :, cols], preferred_element_type=F32)


BLOCK = 32


def inner_kernel(
    x_own, x_peer, small_own, small_peer, mix_own, mix_peer,
    small, normed, middle, middle_normed, weights, wide,
    act, sems, row_sems,
    *, first, taps,
):
    own = lax.axis_index("ch")
    other = 1 - own
    rows = wide.shape[1]
    dilation = first // 2
    reach = taps // 2 * dilation
    count = rows - 2 * reach
    mine = []
    part = first // 2
    for i in range(x_own.shape[0] // first):
        source = x_own.at[pl.ds(pl.multiple_of(i * first + own * part, part), part), :]
        mine.append(pltpu.make_async_copy(source, wide.at[own, pl.ds(i * part, part), :], row_sems.at[i]))
        mine[-1].start()
    copies = []
    for layer in range(2):
        for side, source, at in ((own, mix_own, 0), (other, mix_peer, 1)):
            copies.append(pltpu.make_async_copy(source.at[layer], weights.at[layer, side], sems.at[layer, at]))
            copies[-1].start()
    small[own] = small_own[...]
    small[other] = small_peer[...]
    take_class(wide, other, x_peer, own, first)
    for copy in mine:
        copy.wait()
    for at in range(0, rows, BLOCK):
        here = slice(at, at + BLOCK)
        parts = [wide[h, here, :].astype(F32) for h in range(2)]
        scale = scale_of(parts, None, None)
        for h in range(2):
            normed[h, here, :] = parts[h] * scale * small[h, 0:1, :]
    for at in range(0, count, BLOCK):
        convolve(normed, act, small, 0, at, at, dilation, taps)
    copies[0].wait()
    copies[1].wait()
    for h in range(2):
        middle[h] = wide[h, reach : reach + count, :].astype(F32) + mix(act, weights, 0, count, h)
    for at in range(0, count, BLOCK):
        here = slice(at, at + BLOCK)
        parts = [middle[h, here, :] for h in range(2)]
        scale = scale_of(parts, None, None)
        for h in range(2):
            middle_normed[h, here, :] = parts[h] * scale * small[h, 1:2, :]
    copies[2].wait()
    copies[3].wait()


def tower_kernel(
    near, far, small, inner, inner_middle, inner_normed, weights, inner_wide,
    features, hidden_own, hidden_peer,
    wide, normed, middle, act,
    *, first, second, length, taps,
):
    own = lax.axis_index("ch")
    other = 1 - own
    even = lax.axis_index("seq") % 2 == 0
    width = near.shape[2]
    rows = inner_wide.shape[1]
    start = lax.axis_index("seq") * rows
    length = length // 2
    dilation, wider = first // 2, second // 2
    first_reach = taps // 2 * dilation
    reach1 = taps // 2 * wider
    reach = first_reach + reach1
    done = rows - 2 * first_reach
    lead = rows + 2 * reach1
    upper = reach1 + first_reach

    near_at = jnp.where(even, rows + reach, 0)
    far_at = jnp.where(even, 0, rows + reach)
    for half, side in enumerate((own, other)):
        wide[side, pl.ds(pl.multiple_of(far_at, BLOCK), reach), :] = far[half]
        wide[side, pl.ds(pl.multiple_of(near_at, BLOCK), reach), :] = near[half]
    for h in range(2):
        wide[h, reach : reach + rows, :] = inner_wide[h]
        normed[h, reach : reach + rows, :] = inner[h]

    halo_rows = [*range(0, reach, BLOCK), *range(reach + rows, 2 * reach + rows, BLOCK)]
    for at in halo_rows:
        here = slice(at, at + BLOCK)
        parts = [wide[h, here, :].astype(F32) for h in range(2)]
        scale = scale_of(parts, start - reach + at, length)
        for h in range(2):
            normed[h, here, :] = parts[h] * scale * small[h, 0:1, :]

    still = [*range(0, upper, BLOCK), *range(upper + done, lead, BLOCK)]
    for i, at in enumerate(still):
        convolve(normed, act, small, 0, at, i * BLOCK, dilation, taps)
    for h in range(2):
        middle[h] = mix(act, weights, 0, lead - done, h)

    for i, at in enumerate(still):
        here = slice(i * BLOCK, (i + 1) * BLOCK)
        parts = []
        for h in range(2):
            before = wide[h, first_reach + at : first_reach + at + BLOCK, :].astype(F32)
            parts.append(before + middle[h, here, :])
            middle[h, here, :] = parts[h]
        scale = scale_of(parts, start - reach1 + at, length)
        for h in range(2):
            normed[h, at : at + BLOCK, :] = parts[h] * scale * small[h, 1:2, :]
    for h in range(2):
        normed[h, upper : upper + done, :] = inner_normed[h]
    for at in range(0, rows, BLOCK):
        convolve(normed, act, small, 1, at, at, wider, taps)

    parts = []
    for h in range(2):
        before = jnp.concatenate(
            [middle[h, upper - first_reach : upper, :], inner_middle[h], middle[h, upper : upper + first_reach, :]], axis=0
        )
        parts.append(before + mix(act, weights, 1, rows, h))
        middle[h, 0:rows, :] = parts[h]
    hidden_own[...] = middle[own, 0:rows, :]
    hidden_peer[...] = middle[other, 0:rows, :]
    scale = scale_of(parts, None, None)
    last = 2 + 2 * taps
    for h in range(2):
        features[:, h * width : (h + 1) * width] = (parts[h] * scale * small[h, last : last + 1, :]).astype(BF16)


def project_kernel(own_ref, peer_ref, weight, out):
    count = own_ref.shape[0]
    own = lax.axis_index("ch")
    at = pl.multiple_of(own * count, count)
    back = pl.multiple_of((1 - own) * count, count)
    out[pl.ds(at, count), :] = jnp.dot(own_ref[...], weight[...], preferred_element_type=F32).astype(BF16)
    out[pl.ds(back, count), :] = jnp.dot(peer_ref[...], weight[...], preferred_element_type=F32).astype(BF16)


def halve_kernel(ahead, behind, upper, lower):
    count = upper.shape[0]
    upper[...] = ahead[0:count, :]
    lower[...] = behind[count:, :]


def attend_kernel(*refs, count, scale, first, last):
    q_ref, blocks, refs = refs[0], refs[1 : 1 + count], refs[1 + count :]
    state_in, refs = ((), refs) if first else (refs[:2], refs[2:])
    factor = scale * math.log2(math.e)
    heads = q_ref.shape[1] // HD
    for head in range(heads):
        cols = slice(head * HD, (head + 1) * HD)
        q = q_ref[:, cols]
        scores = [
            lax.dot_general(kv[:, 0:HD], q, (((1,), (1,)), ((), ())), preferred_element_type=F32) for kv in blocks
        ]
        peaks = [jnp.max(s, axis=0, keepdims=True) for s in scores]
        total = None
        context = None
        if not first:
            stats, summed = state_in
            before = stats[head : head + 1, :]
            peaks.append(before)
        peak = functools.reduce(jnp.maximum, peaks)
        if not first:
            keep = jnp.exp2((before - peak) * factor)
            total = stats[heads + head : heads + head + 1, :] * keep
            context = summed[cols, :] * keep
        for s, kv in zip(scores, blocks):
            probs = jnp.exp2((s - peak) * factor)
            part = jnp.sum(probs, axis=0, keepdims=True)
            value = lax.dot_general(
                kv[:, HD:], probs.astype(BF16), (((0,), (0,)), ((), ())), preferred_element_type=F32
            )
            total = part if total is None else total + part
            context = value if context is None else context + value
        if last:
            refs[0][:, cols] = jnp.transpose(context * (1.0 / total)).astype(BF16)
        else:
            refs[0][head : head + 1, :] = peak
            refs[0][heads + head : heads + head + 1, :] = total
            refs[1][cols, :] = context


def begin_kernel(ctx, w_own, hid_own, hid_peer, out):
    count, width = hid_own.shape
    own = lax.axis_index("ch")
    cols = pl.ds(pl.multiple_of(own * width, 128), width)
    for at, hid in ((own * count, hid_own), ((1 - own) * count, hid_peer)):
        rows = pl.ds(pl.multiple_of(at, count), count)
        out[rows, :] = hid[...] + jnp.dot(ctx[rows, :], w_own[:, cols], preferred_element_type=F32)


def finish_kernel(ctx, w_peer, partial, out, staged, sems):
    rows, width = partial.shape
    cols = pl.ds(pl.multiple_of(lax.axis_index("ch") * width, 128), width)
    groups, part = staged.shape[1:3]
    count = rows // 2
    copies = []
    for piece in range(2):
        here = slice(piece * count, (piece + 1) * count)
        mixed = jnp.dot(ctx[here, :], w_peer[:, cols], preferred_element_type=F32)
        value = (partial[here, :] + mixed).astype(BF16)
        for i in range(groups):
            staged[piece, i] = value[i * part : (i + 1) * part, :]
        copies.append(
            pltpu.make_async_copy(staged.at[piece], out.at[:, pl.ds(piece * part, part), :], sems.at[piece])
        )
        copies[-1].start()
    for copy in copies:
        copy.wait()


def bring_kernel(x, to, sem):
    copy = pltpu.make_async_copy(x, to, sem)
    copy.start()
    copy.wait()


def cut_kernel(x_own, x_peer, near, far, sems):
    even = lax.axis_index("seq") % 2 == 0
    count, part = near.shape[1:3]
    last = x_own.shape[0] - count
    rows = pl.ds(pl.multiple_of(lax.axis_index("ch") * part, part), part)
    copies = []
    for half, x in enumerate((x_own, x_peer)):
        for to, begin in ((near, jnp.where(even, last, 0)), (far, jnp.where(even, 0, last))):
            source = x.at[pl.ds(begin, count), rows, :]
            copies.append(pltpu.make_async_copy(source, to.at[half], sems.at[len(copies)]))
            copies[-1].start()
    for copy in copies:
        copy.wait()


def call(kernel, outs, name, mebibytes, *operands, hbm=(), scratch=(), hbm_out=False):
    held, in_specs = [], []
    for i, operand in enumerate(operands):
        in_specs.append(ANY if i in hbm else VMEM)
        held.append(pltpu.with_memory_space_constraint(operand, pltpu.HBM if i in hbm else pltpu.VMEM))
    shapes = tuple((pltpu.HBM if hbm_out else pltpu.VMEM)(shape, dtype) for shape, dtype in outs)
    result = pl.pallas_call(
        kernel,
        out_shape=shapes,
        in_specs=in_specs,
        out_specs=(ANY if hbm_out else VMEM,) * len(shapes),
        scratch_shapes=list(scratch),
        compiler_params=pltpu.CompilerParams(vmem_limit_bytes=mebibytes << 20),
        name=name,
    )(*held)
    return result if len(outs) > 1 else result[0]


def local(seq_in, conv_gain, dw_kernel, mix_weight, attn_gain, q_weight, kv_weight, out_weight):
    rows, width = seq_in.shape
    taps = dw_kernel.shape[1]
    size = lax.axis_size("seq")
    first, second = rows // 8, rows // 4
    first_reach = taps // 2 * first
    reach1 = taps // 2 * second
    reach = first_reach + reach1
    mine = rows // 2
    done = mine - first_reach

    near_pairs = [(i, i ^ 1) for i in range(size)]
    far_pairs = [(0, size - 1), (size - 1, 0)]
    for i in range(1, size - 1, 2):
        far_pairs += [(i, i + 1), (i + 1, i)]
    x_here = call(bring_kernel, [((rows, width), BF16)], "bring", 2, seq_in, hbm=(0,), scratch=[pltpu.SemaphoreType.DMA(())])
    x_peer, x_here, mix_sent, out_sent = lax.optimization_barrier((peer(seq_in), x_here, mix_weight, out_weight))
    groups = rows // first
    cuts = call(
        cut_kernel,
        [((2, reach // first, first // 2, width), BF16)] * 2,
        "cut",
        2,
        x_here.reshape(groups, first, width),
        x_peer.reshape(groups, first, width),
        scratch=[pltpu.SemaphoreType.DMA((4,))],
    )
    to_near, to_far = (part.reshape(2, reach // 2, width) for part in cuts)
    to_near, to_far, mix_sent, out_sent = lax.optimization_barrier((to_near, to_far, mix_sent, out_sent))
    near = lax.ppermute(to_near, "seq", near_pairs)
    far = lax.ppermute(to_far, "seq", far_pairs)

    small = jnp.concatenate(
        [conv_gain, dw_kernel.reshape(2 * taps, width), attn_gain[None, :], jnp.zeros((3, width), F32)], axis=0
    )
    small_peer = peer(small)
    mix_peer = peer(mix_sent)
    out_peer = peer(out_sent)
    kv_flat = kv_weight.reshape(2 * width, 2 * kv_weight.shape[2])

    inner = call(
        functools.partial(inner_kernel, first=first, taps=taps),
        [
            ((2,) + small.shape, F32),
            ((2, mine, width), F32),
            ((2, done, width), F32),
            ((2, done, width), F32),
            ((2, 2, width, 2 * width), BF16),
            ((2, mine, width), BF16),
        ],
        "inner",
        4,
        seq_in, x_peer, small, small_peer, mix_weight, mix_peer,
        hbm=(0, 4, 5),
        scratch=[
            pltpu.VMEM((2, done, width), BF16),
            pltpu.SemaphoreType.DMA((2, 2)),
            pltpu.SemaphoreType.DMA((rows // first,)),
        ],
    )
    near, far, kv_flat, *inner = lax.optimization_barrier((near, far, kv_flat, *inner))

    features, hidden_own, hidden_away = call(
        functools.partial(tower_kernel, first=first, second=second, length=rows * size, taps=taps),
        [((mine, 2 * width), BF16), ((mine, width), F32), ((mine, width), F32)],
        "tower",
        12,
        near, far, *inner,
        scratch=[
            pltpu.VMEM((2, mine + reach, width), BF16),
            pltpu.VMEM((2, mine + reach, width), F32),
            pltpu.VMEM((2, mine + reach1 - done, width), F32),
            pltpu.VMEM((2, mine + reach1 - done, width), BF16),
        ],
    )

    features_peer = peer(features)

    def project(weight, name):
        return call(
            project_kernel, [((rows, weight.shape[1]), BF16)], name, 4, features, features_peer, weight
        )

    kv = project(kv_flat, "keyvalue")
    order = ring_order(size)
    ahead = [(order[i], order[(i + 1) % size]) for i in range(size)]
    behind = [(b, a) for a, b in ahead]
    queries = None
    heads = q_weight.shape[1] // HD
    skip = [(order[i], order[(i + 2) % size]) for i in range(size)]
    skip_back = [(b, a) for a, b in skip]
    attend = functools.partial(attend_kernel, scale=1.0 / math.sqrt(HD))
    hidden_peer = peer(hidden_away)
    state, fresh = (), [kv]
    up = down = kv
    laps = size // 2 - 1
    for step in range(laps + 1):
        if step < laps:
            ahead_of, behind_of = up, down
            up = lax.ppermute(ahead_of, "seq", ahead)
            down = lax.ppermute(behind_of, "seq", behind)
            if step == laps - 1:
                halves = call(halve_kernel, [((rows // 2, kv.shape[1]), BF16)] * 2, "halve", 2, ahead_of, behind_of)
                opposite = [lax.ppermute(halves[0], "seq", skip), lax.ppermute(halves[1], "seq", skip_back)]
        if queries is None:
            queries = project(q_weight, "query")
        state = call(
            functools.partial(attend, count=len(fresh), first=step == 0, last=False),
            [((2 * heads, rows), F32), ((heads * HD, rows), F32)],
            "attend%d" % step,
            8,
            queries, *fresh, *state,
        )
        if step == 0:
            up, hidden_peer, *state = lax.optimization_barrier((up, hidden_peer, *state))
        elif step < laps:
            up, *state = lax.optimization_barrier((up, *state))
        if step < laps:
            down, *state = lax.optimization_barrier((down, *state))
            fresh = [up, down]
    context = call(
        functools.partial(attend, count=len(opposite), first=False, last=True),
        [((rows, heads * HD), BF16)],
        "attend_last",
        8,
        queries, *opposite, *state,
    )
    context_peer = peer(context)
    partial = call(
        begin_kernel, [((rows, width), F32)], "begin", 4, context, out_weight, hidden_own, hidden_peer
    )
    groups = rows // first
    out = call(
        finish_kernel, [((groups, first, width), BF16)], "finish", 4, context_peer, out_peer, partial,
        scratch=[pltpu.VMEM((2, groups, first // 2, width), BF16), pltpu.SemaphoreType.DMA((2,))], hbm_out=True,
    )
    return out.reshape(rows, width)


def solution(mesh):
    return jax.shard_map(
        local,
        mesh=mesh,
        in_specs=(
            P(("grp", "seq"), "ch"),
            P(None, "ch"),
            P(None, None, "ch"),
            P(None, "ch", None),
            P("ch"),
            P(None, "ch"),
            P(None, None, "ch"),
            P("ch", None),
        ),
        out_specs=P(("grp", "seq"), "ch"),
        check_vma=False,
    )
```
